512 devices in a mesh: row: 16 (over x, y_hi), col: 32 (over z, y_lo, core).
Axes of the slice: x: 4, y: 8 (y_hi: 4, y_lo: 2; y = y_hi * 2 + y_lo), z: 8, core: 2. Of those that a mesh axis runs over, the one named last changes fastest.
Arguments:
- left_factor: float32 [8192, 512], P(('row', 'col')), may hold values from -0.0625 to 0.0625
- left_cotangent: float32 [8192, 512], P(('row', 'col')), may hold values from -80 to 80
- right_factor: float32 [24576, 512], P(('col', 'row')), may hold values from -0.0390625 to 0.0390625
- right_cotangent: float32 [24576, 512], P(('col', 'row')), may hold values from -80 to 80
- singular: float32 [512], replicated, may hold values from 0.5 to 2, as said below
- singular_cotangent: float32 [512], replicated, may hold values from -384 to 384
Outputs:
- matrix_cotangent: float32 [8192, 24576], P('row', 'col')
The draws below stay inside these ranges and needn't reach their ends.
Inputs may be any that keep to these rules, and one draw needn't show every extreme that they name: `singular`: strictly decreasing; consecutive values differ by at least 0.75 / 512.
All inputs are finite; a program needn't handle non-finite values.
Results may differ from the reference program's by a relative error of at most 0.0003.
Values sent between devices are 32-bit elements; how exact they have to be, the bound alone decides.
No kernel may reach another device: no remote copies, remote signals or barrier semaphores. Data moves between devices by JAX's collectives and lax.ppermute only.
A program may use at most 64 MiB of HBM per device.

```python
import jax
import jax.numpy as jnp
from jax import lax

K = 512
M = 8192
N = 24576


def draw_singular(key, part):
    jitter = jax.random.uniform(jax.random.fold_in(key, 7), (K,), jnp.float32, 0.0, 0.5)
    steps = jnp.arange(K).astype(jnp.float32)
    return (2.0 - 1.5 * (steps + jitter) / K).astype(jnp.float32)


def spiked(values, own_key, source, target, blocks, factor):
    owner, partner = [(jnp.arange(values.shape[dim]) // (values.shape[dim] // blocks)).reshape([-1 if axis == dim else 1 for axis in range(values.ndim)]) for dim in (source, target)]
    chosen = jax.random.permutation(own_key, blocks)[partner]
    strong = (owner == chosen) | (owner == (partner + blocks // 2) % blocks)
    return jnp.where(strong, factor * values, values)


def block_levels(own_key, shape, shards, least, top_value):
    def one(position, parts):
        heights = jax.random.uniform(jax.random.fold_in(jax.random.fold_in(own_key, 6), position), (parts,), jnp.float32, least / len(shards), top_value / len(shards))
        return jnp.repeat(jnp.exp(heights), shape[position] // parts).reshape((-1,) + (1,) * (len(shape) - position - 1))

    factor_of = one(*shards[0])
    for cut in shards[1:]:
        factor_of = factor_of * one(*cut)
    return factor_of


def scatter_about(own_key, shape, scale, reach, split=(), kind=jnp.bfloat16):
    entries = jax.random.normal(own_key, shape, jnp.float32) * scale
    if len(split) > 0:
        entries = block_levels(own_key, shape, split, -0.22, 0.18) * entries
    return jnp.clip(entries, min=-reach, max=reach).astype(kind)


def gaussian_with(stream_key, extent, deviation, most, split, heavy, held_as=jnp.bfloat16):
    drawn = deviation * jax.random.normal(stream_key, extent, jnp.float32)
    if split:
        drawn = drawn * block_levels(stream_key, extent, split, -0.22, 0.18)
    return jnp.clip(spiked(drawn, jax.random.fold_in(stream_key, 3), *heavy), -most, most).astype(held_as)


def setup_inputs(seed: int = 0) -> dict:
    key_list = jax.random.split(jax.random.key(seed), 7)
    return {
        "left_factor": scatter_about(key_list[0], (M, K), M ** -0.5, 0.0625, ((0, 512),), jnp.float32),
        "left_cotangent": gaussian_with(key_list[1], (M, K), 3.0, 80.0, ((0, 512),), (0, 1, 512, 6.0), jnp.float32),
        "right_factor": scatter_about(key_list[2], (N, K), N ** -0.5, 0.0390625, ((0, 512),), jnp.float32),
        "right_cotangent": gaussian_with(key_list[3], (N, K), 3.0, 80.0, ((0, 512),), (0, 1, 512, 6.0), jnp.float32),
        "singular": draw_singular(jax.random.fold_in(key_list[6], 71), 0),
        "singular_cotangent": scatter_about(key_list[5], (K,), 64.0, 384.0, (), jnp.float32),
    }


def reference(left_factor, left_cotangent, right_factor, right_cotangent, singular, singular_cotangent):
    highest = lax.Precision.HIGHEST
    gram_left = jnp.dot(left_factor.T, left_cotangent, precision=highest, preferred_element_type=jnp.float32)
    gram_right = jnp.dot(right_factor.T, right_cotangent, precision=highest, preferred_element_type=jnp.float32)
    squares = singular * singular
    spread = squares[None, :] - squares[:, None]
    diagonal = jnp.eye(K, dtype=jnp.bool_)
    divided = jnp.where(diagonal, jnp.float32(0.0), 1.0 / jnp.where(diagonal, jnp.float32(1.0), spread))
    inverse = 1.0 / singular
    core = (divided * (gram_left - gram_left.T)) * singular[None, :]
    core = core + jnp.diag(singular_cotangent)
    core = core + singular[:, None] * (divided * (gram_right - gram_right.T))
    core = core - gram_left * inverse[None, :] - inverse[:, None] * gram_right.T
    left_panel = jnp.dot(left_factor, core, precision=highest, preferred_element_type=jnp.float32) + left_cotangent * inverse[None, :]
    scaled_right = right_cotangent * inverse[None, :]
    dims = (((1,), (1,)), ((), ()))
    result = lax.dot_general(left_panel, right_factor, dims, precision=highest, preferred_element_type=jnp.float32)
    result = result + lax.dot_general(left_factor, scaled_right, dims, precision=highest, preferred_element_type=jnp.float32)
    return result
```

```python
import jax
import jax.numpy as jnp
from jax import lax
from jax.sharding import Mesh
from jax.sharding import PartitionSpec as P

ROW = ("x", "yh")
COL = ("z", "yl", "core")
ALL = ROW + COL
SIZES = (4, 4, 8, 2, 2)
HIGHEST = lax.Precision.HIGHEST


def dot(a, b, contract):
    return lax.dot_general(
        a, b, (contract, ((), ())), precision=HIGHEST, preferred_element_type=jnp.float32
    )


def gather(block, axis, size):
    copies = jnp.broadcast_to(block[None], (size,) + block.shape)
    return lax.all_to_all(copies, axis, 0, 0)


def partial_core(left, left_cot, right, right_cot, singular):
    squares = singular * singular
    spread = squares[None, :] - squares[:, None]
    size_k = singular.shape[0]
    diagonal = jnp.eye(size_k, dtype=jnp.bool_)
    divided = jnp.where(
        diagonal, jnp.float32(0.0), 1.0 / jnp.where(diagonal, jnp.float32(1.0), spread)
    )
    inverse = 1.0 / singular
    rows = ((0,), (0,))
    gram_left = dot(left, left_cot, rows)
    gram_left_t = dot(left_cot, left, rows)
    gram_right = dot(right, right_cot, rows)
    gram_right_t = dot(right_cot, right, rows)
    core = divided * (gram_left - gram_left_t) * singular[None, :]
    core = core + singular[:, None] * (divided * (gram_right - gram_right_t))
    return core - gram_left * inverse[None, :] - inverse[:, None] * gram_right_t


def local(left, left_cot, right, right_cot, singular, singular_cot):
    size_k = singular.shape[0]
    inverse = 1.0 / singular
    n_all = 512
    mine = partial_core(left, left_cot, right, right_cot, singular)
    spread_out = lax.all_to_all(mine.reshape(n_all, 4, 128), ALL, 0, 0)

    left_pair = jnp.concatenate([left, left_cot * inverse[None, :]], axis=1)
    right_pair = jnp.concatenate([right_cot * inverse[None, :], right], axis=1)
    lefts = lax.all_gather(left_pair, COL, axis=0, tiled=True)
    rights = lax.all_gather(right_pair, ROW, axis=0, tiled=True)

    row = jnp.sum(spread_out, axis=0)
    core = gather(row, ALL, n_all).reshape(size_k, size_k) + jnp.diag(singular_cot)

    last = ((1,), (1,))
    flat = dot(lefts, rights, last)
    panel = dot(lefts[:, :size_k], core, ((1,), (0,)))
    return flat + dot(panel, rights[:, size_k:], last)


def solution(mesh):
    fine = Mesh(mesh.devices.reshape(SIZES), ALL)
    placed = (
        P(ROW + COL, None),
        P(ROW + COL, None),
        P(COL + ROW, None),
        P(COL + ROW, None),
        P(),
        P(),
    )
    return jax.shard_map(
        local, mesh=fine, in_specs=placed, out_specs=P(ROW, COL), check_vma=False
    )
```

```python
import jax
import jax.numpy as jnp
from jax import lax
from jax.sharding import Mesh
from jax.sharding import PartitionSpec as P

ROW = ("x", "yh")
COL = ("z", "yl", "core")
ALL = ROW + COL
CHIPS = ("x", "yh", "z", "yl")
SIZES = (4, 4, 8, 2, 2)
HIGHEST = lax.Precision.HIGHEST
HIGH = lax.Precision.HIGH
SWAP = [(0, 1), (1, 0)]


def dot(a, b, contract, precision):
    return lax.dot_general(
        a, b, (contract, ((), ())), precision=precision, preferred_element_type=jnp.float32
    )


def gather(block, axis, size):
    copies = jnp.broadcast_to(block[None], (size,) + block.shape)
    return lax.all_to_all(copies, axis, 0, 0)


def swap(block):
    return lax.ppermute(block, "core", SWAP)


def half_core(left, left_cot, right, right_cot, singular, core_index):
    size_k = singular.shape[0]
    half = size_k // 2
    start = core_index * half
    part = lambda a, axis: lax.dynamic_slice_in_dim(a, start, half, axis)
    mine = part(singular, 0)
    spread = (singular * singular)[None, :] - (mine * mine)[:, None]
    diagonal = (start + lax.broadcasted_iota(jnp.int32, (half, size_k), 0)) == (
        lax.broadcasted_iota(jnp.int32, (half, size_k), 1)
    )
    divided = jnp.where(
        diagonal, jnp.float32(0.0), 1.0 / jnp.where(diagonal, jnp.float32(1.0), spread)
    )
    rows = ((0,), (0,))
    gram_left = dot(part(left, 1), left_cot, rows, HIGHEST)
    gram_left_t = dot(part(left_cot, 1), left, rows, HIGHEST)
    gram_right = dot(part(right, 1), right_cot, rows, HIGHEST)
    gram_right_t = dot(part(right_cot, 1), right, rows, HIGHEST)
    across, down = singular[None, :], mine[:, None]
    core = divided * (gram_left * across - gram_left_t * down) * across
    core = core + down * (divided * (gram_right * across - gram_right_t * down))
    return core - gram_left - gram_right_t


def local(left, left_cot, right, right_cot, singular, singular_cot):
    size_k = singular.shape[0]
    n_chips = 256
    half = size_k // 2
    inverse = 1.0 / singular
    core_index = lax.axis_index("core")

    right_pair = jnp.concatenate([right_cot, right], axis=1)
    rights = lax.all_gather(right_pair, ROW, axis=0, tiled=True)

    left_over = left_cot * inverse[None, :]
    left_pair = jnp.concatenate([left, left_over], axis=1)
    lefts = gather(left_pair, ("z", "yl"), 16)
    other_lefts = swap(lefts)

    right_over = right_cot * inverse[None, :]
    sent = jnp.concatenate([left_pair, jnp.concatenate([right, right_over], axis=1)], axis=0)
    got = swap(sent)
    chip_left = jnp.concatenate([sent[:16], got[:16]], axis=0)
    chip_right = jnp.concatenate([sent[16:], got[16:]], axis=0)
    mine = half_core(
        chip_left[:, :size_k],
        chip_left[:, size_k:],
        chip_right[:, :size_k],
        chip_right[:, size_k:],
        singular,
        core_index,
    )
    pieces = lax.all_to_all(mine.reshape(n_chips, 4, 128), CHIPS, 0, 0)
    row = jnp.sum(pieces, axis=0)
    own_half = gather(row, CHIPS, n_chips).reshape(half, size_k)
    other_half = swap(own_half)
    first = core_index == 0
    core = jnp.concatenate(
        [jnp.where(first, own_half, other_half), jnp.where(first, other_half, own_half)], axis=0
    ) + jnp.diag(singular_cot)

    lefts = jnp.stack(
        [jnp.where(first, lefts, other_lefts), jnp.where(first, other_lefts, lefts)], axis=1
    ).reshape(-1, 2 * size_k)
    factor = lefts[:, :size_k]
    last = ((1,), (1,))
    panel = dot(factor, core, ((1,), (0,)), HIGH) + lefts[:, size_k:]
    flat = dot(factor * inverse[None, :], rights[:, :size_k], last, HIGH)
    return flat + dot(panel, rights[:, size_k:], last, HIGH)


def solution(mesh):
    fine = Mesh(mesh.devices.reshape(SIZES), ALL)
    placed = (
        P(ROW + COL, None),
        P(ROW + COL, None),
        P(COL + ROW, None),
        P(COL + ROW, None),
        P(),
        P(),
    )
    return jax.shard_map(
        local, mesh=fine, in_specs=placed, out_specs=P(ROW, COL), check_vma=False
    )
```

```python
import jax
import jax.numpy as jnp
from jax import lax
from jax.sharding import Mesh
from jax.sharding import PartitionSpec as P

ROW = ("x", "yh")
COL = ("z", "yl", "core")
ALL = ROW + COL
PLANE = ("z", "yl")
SIZES = (4, 4, 8, 2, 2)
HIGHEST = lax.Precision.HIGHEST
HIGH = lax.Precision.HIGH
SWAP = [(0, 1), (1, 0)]


def dot(a, b, contract, precision):
    return lax.dot_general(
        a, b, (contract, ((), ())), precision=precision, preferred_element_type=jnp.float32
    )


def gather(block, axis, size):
    copies = jnp.broadcast_to(block[None], (size,) + block.shape)
    return lax.all_to_all(copies, axis, 0, 0)


def swap(block):
    return lax.ppermute(block, "core", SWAP)


def half_core(left, left_cot, right, right_cot, singular, core_index):
    size_k = singular.shape[0]
    half = size_k // 2
    start = core_index * half
    part = lambda a, axis: lax.dynamic_slice_in_dim(a, start, half, axis)
    mine = part(singular, 0)
    spread = (singular * singular)[None, :] - (mine * mine)[:, None]
    diagonal = (start + lax.broadcasted_iota(jnp.int32, (half, size_k), 0)) == (
        lax.broadcasted_iota(jnp.int32, (half, size_k), 1)
    )
    divided = jnp.where(
        diagonal, jnp.float32(0.0), 1.0 / jnp.where(diagonal, jnp.float32(1.0), spread)
    )
    rows = ((0,), (0,))
    gram_left = dot(part(left, 1), left_cot, rows, HIGHEST)
    gram_left_t = dot(part(left_cot, 1), left, rows, HIGHEST)
    gram_right = dot(part(right, 1), right_cot, rows, HIGHEST)
    gram_right_t = dot(part(right_cot, 1), right, rows, HIGHEST)
    across, down = singular[None, :], mine[:, None]
    core = divided * (gram_left * across - gram_left_t * down) * across
    core = core + down * (divided * (gram_right * across - gram_right_t * down))
    return core - gram_left - gram_right_t


def shift(block, axis, size, by):
    return lax.ppermute(block, axis, [(i, (i + by) % size) for i in range(size)])


def near_left(pair):
    at_low = lax.axis_index("yl") == 0
    other = shift(pair, "yl", 2, 1)
    own = jnp.stack([jnp.where(at_low, pair, other), jnp.where(at_low, other, pair)])
    return shift(own, "z", 8, 1), own, shift(own, "z", 8, -1)


def line_left(below, own, above):
    far_below = shift(jnp.stack([below, own, above]), "z", 8, 3)
    far_above = shift(jnp.stack([below, own]), "z", 8, -3)
    ring = [own, above, far_above[0], far_above[1]]
    ring = ring + [far_below[0], far_below[1], far_below[2], below]
    ring = jnp.stack(ring + ring)
    return lax.dynamic_slice_in_dim(ring, 8 - lax.axis_index("z"), 8, 0)


def local(left, left_cot, right, right_cot, singular, singular_cot):
    size_k = singular.shape[0]
    half = size_k // 2
    core_index = lax.axis_index("core")
    first = core_index == 0

    right_pair = jnp.concatenate([right_cot, right], axis=1)
    right_pair, left, left_cot = lax.optimization_barrier((right_pair, left, left_cot))
    rights = lax.all_gather(right_pair, ROW, axis=0, tiled=True)

    inverse = 1.0 / singular
    left_over = left_cot * inverse[None, :]
    right_over = right_cot * inverse[None, :]
    left_pair = jnp.concatenate([left, left_over], axis=1)
    sent = jnp.concatenate([left_pair, jnp.concatenate([right, right_over], axis=1)], axis=0)
    got = swap(sent)
    chip_left = jnp.concatenate([sent[:16], got[:16]], axis=0)
    chip_right = jnp.concatenate([sent[16:], got[16:]], axis=0)
    mine = half_core(
        chip_left[:, :size_k],
        chip_left[:, size_k:],
        chip_right[:, :size_k],
        chip_right[:, size_k:],
        singular,
        core_index,
    )
    pieces = lax.all_to_all(mine.reshape(16, 16, size_k), PLANE, 0, 0)
    near = near_left(left_pair)
    near, rows = lax.optimization_barrier((near, jnp.sum(pieces, axis=0)))
    line = line_left(*near)
    pieces = gather(rows, ROW, 16)
    line, rows = lax.optimization_barrier((line, jnp.sum(pieces, axis=0)))
    line = line.reshape(16, 16, 2 * size_k)
    other_line = swap(line)
    own_half = gather(rows, PLANE, 16).reshape(half, size_k)
    other_half = swap(own_half)
    core = jnp.concatenate(
        [jnp.where(first, own_half, other_half), jnp.where(first, other_half, own_half)], axis=0
    ) + jnp.diag(singular_cot)

    lefts = jnp.stack(
        [jnp.where(first, line, other_line), jnp.where(first, other_line, line)], axis=1
    ).reshape(-1, 2 * size_k)
    factor = lefts[:, :size_k]
    last = ((1,), (1,))
    panel = dot(factor, core, ((1,), (0,)), HIGH) + lefts[:, size_k:]
    flat = dot(factor * inverse[None, :], rights[:, :size_k], last, HIGH)
    return flat + dot(panel, rights[:, size_k:], last, HIGH)


def solution(mesh):
    fine = Mesh(mesh.devices.reshape(SIZES), ALL)
    placed = (
        P(ROW + COL, None),
        P(ROW + COL, None),
        P(COL + ROW, None),
        P(COL + ROW, None),
        P(),
        P(),
    )
    return jax.shard_map(
        local, mesh=fine, in_specs=placed, out_specs=P(ROW, COL), check_vma=False
    )
```

```python
import jax
import jax.numpy as jnp
from jax import lax
from jax.experimental import pallas as pl
from jax.experimental.pallas import tpu as pltpu
from jax.sharding import Mesh
from jax.sharding import PartitionSpec as P

ROW = ("x", "yh")
COL = ("z", "yl", "core")
ALL = ROW + COL
OUTER = ("x", "z")
INNER = ("yh", "yl")
SIZES = (4, 4, 8, 2, 2)
SIZE_K = 512
HALF = 256
HIGHEST = lax.Precision.HIGHEST
HIGH = lax.Precision.HIGH
SWAP = [(0, 1), (1, 0)]


def dot(a, b, contract, precision):
    return lax.dot_general(
        a, b, (contract, ((), ())), precision=precision, preferred_element_type=jnp.float32
    )


def gather(block, axis, size):
    copies = jnp.broadcast_to(block[None], (size,) + block.shape)
    return lax.all_to_all(copies, axis, 0, 0)


def shift(block, axis, size, by):
    return lax.ppermute(block, axis, [(i, (i + by) % size) for i in range(size)])


def swap(block):
    return lax.ppermute(block, "core", SWAP)


def pack_kernel(left, left_cot, right, right_cot, right_pair, left_pair, stacked):
    right_pair[:, :SIZE_K] = right_cot[...]
    right_pair[:, SIZE_K:] = right[...]
    left_pair[:, :SIZE_K] = left[...]
    left_pair[:, SIZE_K:] = left_cot[...]
    stacked[:48, :SIZE_K] = right_cot[...]
    stacked[:48, SIZE_K:] = right[...]
    stacked[48:, :SIZE_K] = left[...]
    stacked[48:, SIZE_K:] = left_cot[...]


def pack(left, left_cot, right, right_cot):
    shapes = ((48, 1024), (16, 1024), (64, 1024))
    return pl.pallas_call(
        pack_kernel,
        out_shape=[jax.ShapeDtypeStruct(s, jnp.float32) for s in shapes],
        cost_estimate=pl.CostEstimate(flops=0, bytes_accessed=1 << 20, transcendentals=0),
        name="pack",
    )(left, left_cot, right, right_cot)


def half_core_kernel(core_index, own, got, s_row, out, lhs, rhs, lhs2, rhs2):
    begin = pl.multiple_of(core_index[0] * HALF, HALF)
    half = pl.ds(begin, HALF)
    cot_half = pl.ds(pl.multiple_of(begin + SIZE_K, HALF), HALF)
    s_all = s_row[...]
    s_half = s_row[:, half]
    inv_all = 1.0 / s_all
    inv_half = 1.0 / s_half
    for i, block in enumerate((own, got)):
        left = pl.ds(16 * i, 16)
        lhs[left, :] = block[48:, half]
        rhs[left, :] = block[48:, SIZE_K:] * s_all
        lhs2[left, :] = block[48:, half]
        rhs2[left, :] = block[48:, SIZE_K:] * inv_all
        left = pl.ds(32 + 16 * i, 16)
        lhs[left, :] = -block[48:, cot_half]
        rhs[left, :] = block[48:, :SIZE_K] * s_all
        right = pl.ds(64 + 48 * i, 48)
        lhs[right, :] = block[:48, cot_half] * s_half
        rhs[right, :] = block[:48, :SIZE_K]
        right = pl.ds(160 + 48 * i, 48)
        lhs[right, :] = -block[:48, half] * s_half
        rhs[right, :] = block[:48, SIZE_K:]
        right = pl.ds(32 + 48 * i, 48)
        lhs2[right, :] = block[:48, half] * inv_half
        rhs2[right, :] = block[:48, SIZE_K:]
    rows = ((0,), (0,))
    eye = lax.broadcasted_iota(jnp.int32, (HALF, HALF), 0) == (
        lax.broadcasted_iota(jnp.int32, (HALF, HALF), 1)
    )
    s_down = jnp.sum(jnp.where(eye, s_half, 0.0), axis=1, keepdims=True)
    spread = s_all * s_all - s_down * s_down
    diagonal = (lax.broadcasted_iota(jnp.int32, (HALF, SIZE_K), 0) + begin) == (
        lax.broadcasted_iota(jnp.int32, (HALF, SIZE_K), 1)
    )
    divided = jnp.where(diagonal, 0.0, 1.0 / jnp.where(diagonal, 1.0, spread))
    main = dot(lhs[...], rhs[...], rows, HIGHEST)
    out[...] = divided * main - dot(lhs2[...], rhs2[...], rows, HIGHEST)


def half_core(core_index, own, got, singular):
    vmem = pl.BlockSpec(memory_space=pltpu.VMEM)
    return pl.pallas_call(
        half_core_kernel,
        out_shape=jax.ShapeDtypeStruct((HALF, SIZE_K), jnp.float32),
        in_specs=[pl.BlockSpec(memory_space=pltpu.SMEM)] + [vmem] * 3,
        out_specs=vmem,
        scratch_shapes=[
            pltpu.VMEM((256, HALF), jnp.float32),
            pltpu.VMEM((256, SIZE_K), jnp.float32),
            pltpu.VMEM((128, HALF), jnp.float32),
            pltpu.VMEM((128, SIZE_K), jnp.float32),
        ],
        cost_estimate=pl.CostEstimate(
            flops=2 * 6 * 384 * HALF * SIZE_K, bytes_accessed=1 << 20, transcendentals=0
        ),
        name="half_core",
    )(core_index.reshape(1), own, got, singular.reshape(1, -1))


def local(left, left_cot, right, right_cot, singular, singular_cot):
    core_index = lax.axis_index("core")
    first = core_index == 0
    at_low = lax.axis_index("yl") == 0

    right_pair, left_pair, stacked = pack(left, left_cot, right, right_cot)
    rights = lax.all_gather(right_pair, ROW, axis=0, tiled=True)
    other = shift(left_pair, "yl", 2, 1)
    got = swap(stacked)
    mine = half_core(core_index, stacked, got, singular)
    pieces = lax.all_to_all(mine.reshape(32, 8, SIZE_K), OUTER, 0, 0)

    own = jnp.stack([jnp.where(at_low, left_pair, other), jnp.where(at_low, other, left_pair)])
    below, above = shift(own, "z", 8, 1), shift(own, "z", 8, -1)

    below, above, rows = lax.optimization_barrier((below, above, jnp.sum(pieces, axis=0)))
    pieces = gather(rows, INNER, 8)
    far_below = shift(jnp.stack([below, own, above]), "z", 8, 3)
    far_above = shift(jnp.stack([below, own]), "z", 8, -3)
    ring = [own[None], above[None], far_above, far_below, below[None]]
    line = jnp.concatenate(ring + ring, axis=0)
    line = lax.dynamic_slice_in_dim(line, 8 - lax.axis_index("z"), 8, 0).reshape(16, 16, 1024)

    line, rows = lax.optimization_barrier((line, jnp.sum(pieces, axis=0)))
    own_half = gather(rows, OUTER, 32).reshape(HALF, SIZE_K)
    other_line = swap(line)
    lefts = jnp.stack(
        [jnp.where(first, line, other_line), jnp.where(first, other_line, line)], axis=1
    ).reshape(-1, 1024)
    other_half = swap(own_half)
    core = jnp.concatenate(
        [jnp.where(first, own_half, other_half), jnp.where(first, other_half, own_half)], axis=0
    ) + jnp.diag(singular_cot)

    inverse = (1.0 / singular)[None, :]
    factor = lefts[:, :SIZE_K]
    last = ((1,), (1,))
    panel = dot(factor, core, ((1,), (0,)), HIGH) + lefts[:, SIZE_K:] * inverse
    flat = dot(factor * inverse, rights[:, :SIZE_K], last, HIGH)
    return flat + dot(panel, rights[:, SIZE_K:], last, HIGH)


def solution(mesh):
    fine = Mesh(mesh.devices.reshape(SIZES), ALL)
    placed = (
        P(ROW + COL, None),
        P(ROW + COL, None),
        P(COL + ROW, None),
        P(COL + ROW, None),
        P(),
        P(),
    )
    return jax.shard_map(local, mesh=fine, in_specs=placed, out_specs=P(ROW, COL), check_vma=False)
```

```python
import jax
import jax.numpy as jnp
from jax import lax
from jax.experimental import pallas as pl
from jax.experimental.pallas import tpu as pltpu
from jax.sharding import Mesh
from jax.sharding import PartitionSpec as P

ROW = ("x", "yh")
COL = ("z", "yl", "core")
ALL = ROW + COL
OUTER = ("x", "z")
INNER = ("yh", "yl")
SIZES = (4, 4, 8, 2, 2)
SIZE_K = 512
HALF = 256
HIGHEST = lax.Precision.HIGHEST
HIGH = lax.Precision.HIGH
SWAP = [(0, 1), (1, 0)]


def dot(a, b, contract, precision):
    return lax.dot_general(
        a, b, (contract, ((), ())), precision=precision, preferred_element_type=jnp.float32
    )


def gather(block, axis, size):
    copies = jnp.broadcast_to(block[None], (size,) + block.shape)
    return lax.all_to_all(copies, axis, 0, 0)


def shift(block, axis, size, by):
    return lax.ppermute(block, axis, [(i, (i + by) % size) for i in range(size)])


def swap(block):
    return lax.ppermute(block, "core", SWAP)


def pack_kernel(left, left_cot, right, right_cot, right_pair, left_pair, stacked):
    right_pair[:, :SIZE_K] = right_cot[...]
    right_pair[:, SIZE_K:] = right[...]
    left_pair[:, :SIZE_K] = left[...]
    left_pair[:, SIZE_K:] = left_cot[...]
    stacked[:48, :SIZE_K] = right_cot[...]
    stacked[:48, SIZE_K:] = right[...]
    stacked[48:, :SIZE_K] = left[...]
    stacked[48:, SIZE_K:] = left_cot[...]


def pack(left, left_cot, right, right_cot):
    shapes = ((48, 1024), (16, 1024), (64, 1024))
    return pl.pallas_call(
        pack_kernel,
        out_shape=[jax.ShapeDtypeStruct(s, jnp.float32) for s in shapes],
        cost_estimate=pl.CostEstimate(flops=0, bytes_accessed=1 << 20, transcendentals=0),
        name="pack",
    )(left, left_cot, right, right_cot)


def half_core_kernel(core_index, own, got, s_row, out, lhs, rhs, lhs2, rhs2):
    begin = pl.multiple_of(core_index[0] * HALF, HALF)
    half = pl.ds(begin, HALF)
    cot_half = pl.ds(pl.multiple_of(begin + SIZE_K, HALF), HALF)
    s_all = s_row[...]
    s_half = s_row[:, half]
    inv_all = 1.0 / s_all
    inv_half = 1.0 / s_half
    for i, block in enumerate((own, got)):
        left = pl.ds(16 * i, 16)
        lhs[left, :] = block[48:, half]
        rhs[left, :] = block[48:, SIZE_K:] * s_all
        lhs2[left, :] = block[48:, half]
        rhs2[left, :] = block[48:, SIZE_K:] * inv_all
        left = pl.ds(32 + 16 * i, 16)
        lhs[left, :] = -block[48:, cot_half]
        rhs[left, :] = block[48:, :SIZE_K] * s_all
        right = pl.ds(64 + 48 * i, 48)
        lhs[right, :] = block[:48, cot_half] * s_half
        rhs[right, :] = block[:48, :SIZE_K]
        right = pl.ds(160 + 48 * i, 48)
        lhs[right, :] = -block[:48, half] * s_half
        rhs[right, :] = block[:48, SIZE_K:]
        right = pl.ds(32 + 48 * i, 48)
        lhs2[right, :] = block[:48, half] * inv_half
        rhs2[right, :] = block[:48, SIZE_K:]
    rows = ((0,), (0,))
    eye = lax.broadcasted_iota(jnp.int32, (HALF, HALF), 0) == (
        lax.broadcasted_iota(jnp.int32, (HALF, HALF), 1)
    )
    s_down = jnp.sum(jnp.where(eye, s_half, 0.0), axis=1, keepdims=True)
    spread = s_all * s_all - s_down * s_down
    diagonal = (lax.broadcasted_iota(jnp.int32, (HALF, SIZE_K), 0) + begin) == (
        lax.broadcasted_iota(jnp.int32, (HALF, SIZE_K), 1)
    )
    divided = jnp.where(diagonal, 0.0, 1.0 / jnp.where(diagonal, 1.0, spread))
    main = dot(lhs[...], rhs[...], rows, HIGHEST)
    out[...] = divided * main - dot(lhs2[...], rhs2[...], rows, HIGHEST)


def half_core(core_index, own, got, singular):
    vmem = pl.BlockSpec(memory_space=pltpu.VMEM)
    return pl.pallas_call(
        half_core_kernel,
        out_shape=jax.ShapeDtypeStruct((HALF, SIZE_K), jnp.float32),
        in_specs=[pl.BlockSpec(memory_space=pltpu.SMEM)] + [vmem] * 3,
        out_specs=vmem,
        scratch_shapes=[
            pltpu.VMEM((256, HALF), jnp.float32),
            pltpu.VMEM((256, SIZE_K), jnp.float32),
            pltpu.VMEM((128, HALF), jnp.float32),
            pltpu.VMEM((128, SIZE_K), jnp.float32),
        ],
        cost_estimate=pl.CostEstimate(
            flops=2 * 6 * 384 * HALF * SIZE_K, bytes_accessed=1 << 20, transcendentals=0
        ),
        name="half_core",
    )(core_index.reshape(1), own, got, singular.reshape(1, -1))


def local(left, left_cot, right, right_cot, singular, singular_cot):
    core_index = lax.axis_index("core")
    first = core_index == 0
    at_low = lax.axis_index("yl") == 0

    right_pair, left_pair, stacked = pack(left, left_cot, right, right_cot)
    rights = lax.all_gather(right_pair, ROW, axis=0, tiled=True)
    other = shift(left_pair, "yl", 2, 1)
    got = swap(stacked)
    mine = half_core(core_index, stacked, got, singular)
    pieces = lax.all_to_all(mine.reshape(32, 8, SIZE_K), OUTER, 0, 0)

    own = jnp.stack([jnp.where(at_low, left_pair, other), jnp.where(at_low, other, left_pair)])
    below, above = shift(own, "z", 8, 1), shift(own, "z", 8, -1)

    below, above, rows = lax.optimization_barrier((below, above, jnp.sum(pieces, axis=0)))
    pieces = gather(rows, INNER, 8)
    mid_below = shift(jnp.stack([below, own]), "z", 8, 2)
    mid_above = shift(jnp.stack([own, above]), "z", 8, -2)
    last_above = shift(mid_above[1], "z", 8, -1)
    ring = [own[None], above[None], mid_above, last_above[None], mid_below, below[None]]
    line = jnp.concatenate(ring + ring, axis=0)
    line = lax.dynamic_slice_in_dim(line, 8 - lax.axis_index("z"), 8, 0)
    line = line.reshape(16, 16, 1024)
    rows = jnp.sum(pieces, axis=0)
    own_half = gather(rows, OUTER, 32).reshape(HALF, SIZE_K)
    other_line = swap(line)
    lefts = jnp.stack(
        [jnp.where(first, line, other_line), jnp.where(first, other_line, line)], axis=1
    ).reshape(-1, 1024)
    other_half = swap(own_half)
    core = jnp.concatenate(
        [jnp.where(first, own_half, other_half), jnp.where(first, other_half, own_half)], axis=0
    ) + jnp.diag(singular_cot)

    inverse = (1.0 / singular)[None, :]
    factor = lefts[:, :SIZE_K]
    last = ((1,), (1,))
    panel = dot(factor, core, ((1,), (0,)), HIGH) + lefts[:, SIZE_K:] * inverse
    flat = dot(factor * inverse, rights[:, :SIZE_K], last, HIGH)
    flat = lax.optimization_barrier(flat)
    return flat + dot(panel, rights[:, SIZE_K:], last, HIGH)


def solution(mesh):
    fine = Mesh(mesh.devices.reshape(SIZES), ALL)
    placed = (
        P(ROW + COL, None),
        P(ROW + COL, None),
        P(COL + ROW, None),
        P(COL + ROW, None),
        P(),
        P(),
    )
    return jax.shard_map(local, mesh=fine, in_specs=placed, out_specs=P(ROW, COL), check_vma=False)
```

```python
import jax
import jax.numpy as jnp
from jax import lax
from jax.experimental import pallas as pl
from jax.experimental.pallas import tpu as pltpu
from jax.sharding import Mesh
from jax.sharding import PartitionSpec as P

ROW = ("x", "yh")
COL = ("z", "yl", "core")
ALL = ROW + COL
OUTER = ("x", "z")
INNER = ("yh", "yl")
SIZES = (4, 4, 8, 2, 2)
SIZE_K = 512
HALF = 256
HIGHEST = lax.Precision.HIGHEST
HIGH = lax.Precision.HIGH
SWAP = [(0, 1), (1, 0)]


def dot(a, b, contract, precision):
    return lax.dot_general(
        a, b, (contract, ((), ())), precision=precision, preferred_element_type=jnp.float32
    )


def gather(block, axis, size):
    copies = jnp.broadcast_to(block[None], (size,) + block.shape)
    return lax.all_to_all(copies, axis, 0, 0)


def shift(block, axis, size, by):
    return lax.ppermute(block, axis, [(i, (i + by) % size) for i in range(size)])


def swap(block):
    return lax.ppermute(block, "core", SWAP)


def pack_kernel(left, left_cot, right, right_cot, right_pair, left_pair, stacked, held, sems):
    low, high = pl.ds(0, SIZE_K), pl.ds(SIZE_K, SIZE_K)
    top, bottom = pl.ds(0, 48), pl.ds(48, 16)

    def start(i, source, target):
        copy = pltpu.make_async_copy(source, target, sems.at[i])
        copy.start()
        return copy

    reads = [
        start(0, right_cot, held.at[top, low]),
        start(1, right, held.at[top, high]),
        start(2, left, held.at[bottom, low]),
        start(3, left_cot, held.at[bottom, high]),
    ]
    for copy in reads:
        copy.wait()
    writes = [
        start(4, held, stacked),
        start(5, held.at[top, :], right_pair),
        start(6, held.at[bottom, :], left_pair),
    ]
    for copy in writes:
        copy.wait()


def pack(left, left_cot, right, right_cot):
    shapes = ((48, 1024), (16, 1024), (64, 1024))
    hbm = pl.BlockSpec(memory_space=pl.ANY)
    return pl.pallas_call(
        pack_kernel,
        out_shape=[jax.ShapeDtypeStruct(s, jnp.float32) for s in shapes],
        in_specs=[hbm] * 4,
        out_specs=[hbm] * 3,
        scratch_shapes=[
            pltpu.VMEM((64, 1024), jnp.float32),
            pltpu.SemaphoreType.DMA((7,)),
        ],
        cost_estimate=pl.CostEstimate(flops=0, bytes_accessed=1 << 20, transcendentals=0),
        name="pack",
    )(left, left_cot, right, right_cot)


def half_core_kernel(core_index, own, got, s_row, out, lhs, rhs, lhs2, rhs2):
    begin = pl.multiple_of(core_index[0] * HALF, HALF)
    half = pl.ds(begin, HALF)
    cot_half = pl.ds(pl.multiple_of(begin + SIZE_K, HALF), HALF)
    s_all = s_row[...]
    s_half = s_row[:, half]
    inv_all = 1.0 / s_all
    inv_half = 1.0 / s_half
    for i, block in enumerate((own, got)):
        left = pl.ds(16 * i, 16)
        lhs[left, :] = block[48:, half]
        rhs[left, :] = block[48:, SIZE_K:] * s_all
        lhs2[left, :] = block[48:, half]
        rhs2[left, :] = block[48:, SIZE_K:] * inv_all
        left = pl.ds(32 + 16 * i, 16)
        lhs[left, :] = -block[48:, cot_half]
        rhs[left, :] = block[48:, :SIZE_K] * s_all
        right = pl.ds(64 + 48 * i, 48)
        lhs[right, :] = block[:48, cot_half] * s_half
        rhs[right, :] = block[:48, :SIZE_K]
        right = pl.ds(160 + 48 * i, 48)
        lhs[right, :] = -block[:48, half] * s_half
        rhs[right, :] = block[:48, SIZE_K:]
        right = pl.ds(32 + 48 * i, 48)
        lhs2[right, :] = block[:48, half] * inv_half
        rhs2[right, :] = block[:48, SIZE_K:]
    rows = ((0,), (0,))
    eye = lax.broadcasted_iota(jnp.int32, (HALF, HALF), 0) == (
        lax.broadcasted_iota(jnp.int32, (HALF, HALF), 1)
    )
    s_down = jnp.sum(jnp.where(eye, s_half, 0.0), axis=1, keepdims=True)
    spread = s_all * s_all - s_down * s_down
    diagonal = (lax.broadcasted_iota(jnp.int32, (HALF, SIZE_K), 0) + begin) == (
        lax.broadcasted_iota(jnp.int32, (HALF, SIZE_K), 1)
    )
    divided = jnp.where(diagonal, 0.0, 1.0 / jnp.where(diagonal, 1.0, spread))
    main = dot(lhs[...], rhs[...], rows, HIGHEST)
    out[...] = divided * main - dot(lhs2[...], rhs2[...], rows, HIGHEST)


def half_core(core_index, own, got, singular):
    vmem = pl.BlockSpec(memory_space=pltpu.VMEM)
    return pl.pallas_call(
        half_core_kernel,
        out_shape=jax.ShapeDtypeStruct((HALF, SIZE_K), jnp.float32),
        in_specs=[pl.BlockSpec(memory_space=pltpu.SMEM)] + [vmem] * 3,
        out_specs=vmem,
        scratch_shapes=[
            pltpu.VMEM((256, HALF), jnp.float32),
            pltpu.VMEM((256, SIZE_K), jnp.float32),
            pltpu.VMEM((128, HALF), jnp.float32),
            pltpu.VMEM((128, SIZE_K), jnp.float32),
        ],
        cost_estimate=pl.CostEstimate(
            flops=2 * 6 * 384 * HALF * SIZE_K, bytes_accessed=1 << 20, transcendentals=0
        ),
        compiler_params=pltpu.CompilerParams(vmem_limit_bytes=12 << 20),
        name="half_core",
    )(core_index.reshape(1), own, got, singular.reshape(1, -1))


def place_kernel(z, below, own, above, mid_below, mid_above, last_above, out):
    blocks = [own[...], above[...], mid_above[0], mid_above[1], last_above[...]]
    blocks = blocks + [mid_below[0], mid_below[1], below[...]]
    for i, block in enumerate(blocks):
        out[lax.rem(z[0] + i, 8)] = block


def place(z, *blocks):
    vmem = pl.BlockSpec(memory_space=pltpu.VMEM)
    return pl.pallas_call(
        place_kernel,
        out_shape=jax.ShapeDtypeStruct((8,) + blocks[1].shape, jnp.float32),
        in_specs=[pl.BlockSpec(memory_space=pltpu.SMEM)] + [vmem] * 6,
        out_specs=vmem,
        cost_estimate=pl.CostEstimate(flops=0, bytes_accessed=2 << 20, transcendentals=0),
        compiler_params=pltpu.CompilerParams(vmem_limit_bytes=8 << 20),
        name="place",
    )(z.reshape(1), *blocks)


def local(left, left_cot, right, right_cot, singular, singular_cot):
    core_index = lax.axis_index("core")
    first = core_index == 0
    at_low = lax.axis_index("yl") == 0

    right_pair, left_pair, stacked = pack(left, left_cot, right, right_cot)
    rights = lax.all_gather(right_pair, ROW, axis=0, tiled=True)
    other = shift(left_pair, "yl", 2, 1)
    got = swap(stacked)
    mine = half_core(core_index, stacked, got, singular)
    pieces = lax.all_to_all(mine.reshape(32, 8, SIZE_K), OUTER, 0, 0)

    own = jnp.stack([jnp.where(at_low, left_pair, other), jnp.where(at_low, other, left_pair)])
    below, above = shift(own, "z", 8, 1), shift(own, "z", 8, -1)

    mid_below = shift(jnp.stack([below, own]), "z", 8, 2)
    mid_above = shift(jnp.stack([own, above]), "z", 8, -2)
    pieces = gather(jnp.sum(pieces, axis=0), INNER, 8)
    last_above = shift(mid_above[1], "z", 8, -1)
    line = place(lax.axis_index("z"), below, own, above, mid_below, mid_above, last_above)
    line = line.reshape(16, 16, 1024)
    rows = jnp.sum(pieces, axis=0)
    own_half = gather(rows, OUTER, 32).reshape(HALF, SIZE_K)
    other_line = swap(line)
    lefts = jnp.stack(
        [jnp.where(first, line, other_line), jnp.where(first, other_line, line)], axis=1
    ).reshape(-1, 1024)
    other_half = swap(own_half)
    core = jnp.concatenate(
        [jnp.where(first, own_half, other_half), jnp.where(first, other_half, own_half)], axis=0
    ) + jnp.diag(singular_cot)

    inverse = (1.0 / singular)[None, :]
    factor = lefts[:, :SIZE_K]
    last = ((1,), (1,))
    panel = dot(factor, core, ((1,), (0,)), HIGH) + lefts[:, SIZE_K:] * inverse
    flat = dot(factor * inverse, rights[:, :SIZE_K], last, HIGH)
    flat = lax.optimization_barrier(flat)
    return flat + dot(panel, rights[:, SIZE_K:], last, HIGH)


def solution(mesh):
    fine = Mesh(mesh.devices.reshape(SIZES), ALL)
    placed = (
        P(ROW + COL, None),
        P(ROW + COL, None),
        P(COL + ROW, None),
        P(COL + ROW, None),
        P(),
        P(),
    )
    return jax.shard_map(local, mesh=fine, in_specs=placed, out_specs=P(ROW, COL), check_vma=False)
```

```python
import jax
import jax.numpy as jnp
from jax import lax
from jax.experimental import pallas as pl
from jax.experimental.pallas import tpu as pltpu
from jax.sharding import Mesh
from jax.sharding import PartitionSpec as P

ROW = ("x", "yh")
COL = ("z", "yl", "core")
ALL = ROW + COL
OUTER = ("x", "z")
INNER = ("yh", "yl")
SIZES = (4, 4, 8, 2, 2)
SIZE_K = 512
HALF = 256
HIGHEST = lax.Precision.HIGHEST
HIGH = lax.Precision.HIGH
SWAP = [(0, 1), (1, 0)]


def dot(a, b, contract, precision):
    return lax.dot_general(
        a, b, (contract, ((), ())), precision=precision, preferred_element_type=jnp.float32
    )


def gather(block, axis, size):
    copies = jnp.broadcast_to(block[None], (size,) + block.shape)
    return lax.all_to_all(copies, axis, 0, 0)


def shift(block, axis, size, by):
    return lax.ppermute(block, axis, [(i, (i + by) % size) for i in range(size)])


def swap(block):
    return lax.ppermute(block, "core", SWAP)


def pack_kernel(left, left_cot, right, right_cot, right_pair, left_pair, stacked, held, sems):
    low, high = pl.ds(0, SIZE_K), pl.ds(SIZE_K, SIZE_K)
    top, bottom = pl.ds(0, 48), pl.ds(48, 16)

    def start(i, source, target):
        copy = pltpu.make_async_copy(source, target, sems.at[i])
        copy.start()
        return copy

    reads = [
        start(0, right_cot, held.at[top, low]),
        start(1, right, held.at[top, high]),
        start(2, left, held.at[bottom, low]),
        start(3, left_cot, held.at[bottom, high]),
    ]
    for copy in reads:
        copy.wait()
    writes = [
        start(4, held, stacked),
        start(5, held.at[top, :], right_pair),
        start(6, held.at[bottom, :], left_pair),
    ]
    for copy in writes:
        copy.wait()


def pack(left, left_cot, right, right_cot):
    shapes = ((48, 1024), (16, 1024), (64, 1024))
    hbm = pl.BlockSpec(memory_space=pl.ANY)
    return pl.pallas_call(
        pack_kernel,
        out_shape=[jax.ShapeDtypeStruct(s, jnp.float32) for s in shapes],
        in_specs=[hbm] * 4,
        out_specs=[hbm] * 3,
        scratch_shapes=[
            pltpu.VMEM((64, 1024), jnp.float32),
            pltpu.SemaphoreType.DMA((7,)),
        ],
        cost_estimate=pl.CostEstimate(flops=0, bytes_accessed=1 << 20, transcendentals=0),
        name="pack",
    )(left, left_cot, right, right_cot)


def half_core_kernel(core_index, own, got, s_row, out, lhs, rhs, lhs2, rhs2):
    begin = pl.multiple_of(core_index[0] * HALF, HALF)
    half = pl.ds(begin, HALF)
    cot_half = pl.ds(pl.multiple_of(begin + SIZE_K, HALF), HALF)
    s_all = s_row[...]
    s_half = s_row[:, half]
    inv_all = 1.0 / s_all
    inv_half = 1.0 / s_half
    for i, block in enumerate((own, got)):
        left = pl.ds(16 * i, 16)
        lhs[left, :] = block[48:, half]
        rhs[left, :] = block[48:, SIZE_K:] * s_all
        lhs2[left, :] = block[48:, half]
        rhs2[left, :] = block[48:, SIZE_K:] * inv_all
        left = pl.ds(32 + 16 * i, 16)
        lhs[left, :] = -block[48:, cot_half]
        rhs[left, :] = block[48:, :SIZE_K] * s_all
        right = pl.ds(64 + 48 * i, 48)
        lhs[right, :] = block[:48, cot_half] * s_half
        rhs[right, :] = block[:48, :SIZE_K]
        right = pl.ds(160 + 48 * i, 48)
        lhs[right, :] = -block[:48, half] * s_half
        rhs[right, :] = block[:48, SIZE_K:]
        right = pl.ds(32 + 48 * i, 48)
        lhs2[right, :] = block[:48, half] * inv_half
        rhs2[right, :] = block[:48, SIZE_K:]
    rows = ((0,), (0,))
    eye = lax.broadcasted_iota(jnp.int32, (HALF, HALF), 0) == (
        lax.broadcasted_iota(jnp.int32, (HALF, HALF), 1)
    )
    s_down = jnp.sum(jnp.where(eye, s_half, 0.0), axis=1, keepdims=True)
    spread = s_all * s_all - s_down * s_down
    diagonal = (lax.broadcasted_iota(jnp.int32, (HALF, SIZE_K), 0) + begin) == (
        lax.broadcasted_iota(jnp.int32, (HALF, SIZE_K), 1)
    )
    divided = jnp.where(diagonal, 0.0, 1.0 / jnp.where(diagonal, 1.0, spread))
    main = dot(lhs[...], rhs[...], rows, HIGHEST)
    out[...] = divided * main - dot(lhs2[...], rhs2[...], rows, HIGHEST)


def half_core(core_index, own, got, singular):
    vmem = pl.BlockSpec(memory_space=pltpu.VMEM)
    return pl.pallas_call(
        half_core_kernel,
        out_shape=jax.ShapeDtypeStruct((HALF, SIZE_K), jnp.float32),
        in_specs=[pl.BlockSpec(memory_space=pltpu.SMEM)] + [vmem] * 3,
        out_specs=vmem,
        scratch_shapes=[
            pltpu.VMEM((256, HALF), jnp.float32),
            pltpu.VMEM((256, SIZE_K), jnp.float32),
            pltpu.VMEM((128, HALF), jnp.float32),
            pltpu.VMEM((128, SIZE_K), jnp.float32),
        ],
        cost_estimate=pl.CostEstimate(
            flops=2 * 6 * 384 * HALF * SIZE_K, bytes_accessed=1 << 20, transcendentals=0
        ),
        compiler_params=pltpu.CompilerParams(vmem_limit_bytes=12 << 20),
        name="half_core",
    )(core_index.reshape(1), own, got, singular.reshape(1, -1))


def place_kernel(z, below, own, above, mid_below, mid_above, last_above, out):
    blocks = [own[...], above[...], mid_above[0], mid_above[1], last_above[...]]
    blocks = blocks + [mid_below[0], mid_below[1], below[...]]
    for i, block in enumerate(blocks):
        out[lax.rem(z[0] + i, 8)] = block


def merge_kernel(index, mine, theirs, out):
    out[:, index[0]] = mine[...]
    out[:, 1 - index[0]] = theirs[...]


def assemble(kernel, shape, index, *blocks):
    vmem = pl.BlockSpec(memory_space=pltpu.VMEM)
    return pl.pallas_call(
        kernel,
        out_shape=jax.ShapeDtypeStruct(shape, jnp.float32),
        in_specs=[pl.BlockSpec(memory_space=pltpu.SMEM)] + [vmem] * len(blocks),
        out_specs=vmem,
        cost_estimate=pl.CostEstimate(flops=0, bytes_accessed=2 << 20, transcendentals=0),
        compiler_params=pltpu.CompilerParams(vmem_limit_bytes=10 << 20),
    )(index.reshape(1), *blocks)


def local(left, left_cot, right, right_cot, singular, singular_cot):
    core_index = lax.axis_index("core")
    first = core_index == 0

    right_pair, left_pair, stacked = pack(left, left_cot, right, right_cot)
    rights = lax.all_gather(right_pair, ROW, axis=0, tiled=True)
    got = swap(stacked)
    mine = half_core(core_index, stacked, got, singular)
    pieces = lax.all_to_all(mine.reshape(32, 8, SIZE_K), OUTER, 0, 0)

    own = left_pair
    below, above = shift(own, "z", 8, 1), shift(own, "z", 8, -1)
    mid_below = shift(jnp.stack([below, own]), "z", 8, 2)
    mid_above = shift(jnp.stack([own, above]), "z", 8, -2)
    pieces = gather(jnp.sum(pieces, axis=0), INNER, 8)
    last_above = shift(mid_above[1], "z", 8, -1)
    blocks = (below, own, above, mid_below, mid_above, last_above)
    line = assemble(place_kernel, (8, 16, 1024), lax.axis_index("z"), *blocks)
    other_line = shift(line, "yl", 2, 1)
    plane = assemble(merge_kernel, (8, 2, 16, 1024), lax.axis_index("yl"), line, other_line)
    plane = plane.reshape(16, 16, 1024)
    rows = jnp.sum(pieces, axis=0)
    own_half = gather(rows, OUTER, 32).reshape(HALF, SIZE_K)
    other_plane = swap(plane)
    lefts = assemble(
        merge_kernel, (16, 2, 16, 1024), core_index, plane, other_plane
    ).reshape(-1, 1024)
    other_half = swap(own_half)
    core = jnp.concatenate(
        [jnp.where(first, own_half, other_half), jnp.where(first, other_half, own_half)], axis=0
    ) + jnp.diag(singular_cot)

    inverse = (1.0 / singular)[None, :]
    factor = lefts[:, :SIZE_K]
    last = ((1,), (1,))
    panel = dot(factor, core, ((1,), (0,)), HIGH) + lefts[:, SIZE_K:] * inverse
    flat = dot(factor * inverse, rights[:, :SIZE_K], last, HIGH)
    flat = lax.optimization_barrier(flat)
    return flat + dot(panel, rights[:, SIZE_K:], last, HIGH)


def solution(mesh):
    fine = Mesh(mesh.devices.reshape(SIZES), ALL)
    placed = (
        P(ROW + COL, None),
        P(ROW + COL, None),
        P(COL + ROW, None),
        P(COL + ROW, None),
        P(),
        P(),
    )
    return jax.shard_map(local, mesh=fine, in_specs=placed, out_specs=P(ROW, COL), check_vma=False)
```

```python
import jax
import jax.numpy as jnp
from jax import lax
from jax.experimental import pallas as pl
from jax.experimental.pallas import tpu as pltpu
from jax.sharding import Mesh
from jax.sharding import PartitionSpec as P

ROW = ("x", "yh")
COL = ("zh", "zl", "yl", "core")
ALL = ROW + COL
Z = ("zh", "zl")
OUTER = ("x", "zl", "yl")
INNER = ("yh", "zh")
SIZES = (4, 4, 4, 2, 2, 2)
SIZE_K = 512
HALF = 256
HIGHEST = lax.Precision.HIGHEST
HIGH = lax.Precision.HIGH
SWAP = [(0, 1), (1, 0)]


def dot(a, b, contract, precision):
    return lax.dot_general(
        a, b, (contract, ((), ())), precision=precision, preferred_element_type=jnp.float32
    )


def gather(block, axis, size):
    copies = jnp.broadcast_to(block[None], (size,) + block.shape)
    return lax.all_to_all(copies, axis, 0, 0)


def shift(block, axis, size, by):
    return lax.ppermute(block, axis, [(i, (i + by) % size) for i in range(size)])


def swap(block):
    return lax.ppermute(block, "core", SWAP)


def pack_kernel(left, left_cot, right, right_cot, right_pair, left_pair, stacked, held, sems):
    low, high = pl.ds(0, SIZE_K), pl.ds(SIZE_K, SIZE_K)
    top, bottom = pl.ds(0, 48), pl.ds(48, 16)

    def start(i, source, target):
        copy = pltpu.make_async_copy(source, target, sems.at[i])
        copy.start()
        return copy

    reads = [
        start(0, right_cot, held.at[top, low]),
        start(1, right, held.at[top, high]),
        start(2, left, held.at[bottom, low]),
        start(3, left_cot, held.at[bottom, high]),
    ]
    for copy in reads:
        copy.wait()
    writes = [
        start(4, held, stacked),
        start(5, held.at[top, :], right_pair),
        start(6, held.at[bottom, :], left_pair),
    ]
    for copy in writes:
        copy.wait()


def pack(left, left_cot, right, right_cot):
    shapes = ((48, 1024), (16, 1024), (64, 1024))
    hbm = pl.BlockSpec(memory_space=pl.ANY)
    return pl.pallas_call(
        pack_kernel,
        out_shape=[jax.ShapeDtypeStruct(s, jnp.float32) for s in shapes],
        in_specs=[hbm] * 4,
        out_specs=[hbm] * 3,
        scratch_shapes=[
            pltpu.VMEM((64, 1024), jnp.float32),
            pltpu.SemaphoreType.DMA((7,)),
        ],
        cost_estimate=pl.CostEstimate(flops=0, bytes_accessed=1 << 20, transcendentals=0),
        name="pack",
    )(left, left_cot, right, right_cot)


def half_core_kernel(core_index, own, got, s_row, out, lhs, rhs, lhs2, rhs2):
    begin = pl.multiple_of(core_index[0] * HALF, HALF)
    half = pl.ds(begin, HALF)
    cot_half = pl.ds(pl.multiple_of(begin + SIZE_K, HALF), HALF)
    s_all = s_row[...]
    s_half = s_row[:, half]
    inv_all = 1.0 / s_all
    inv_half = 1.0 / s_half
    for i, block in enumerate((own, got)):
        left = pl.ds(16 * i, 16)
        lhs[left, :] = block[48:, half]
        rhs[left, :] = block[48:, SIZE_K:] * s_all
        lhs2[left, :] = block[48:, half]
        rhs2[left, :] = block[48:, SIZE_K:] * inv_all
        left = pl.ds(32 + 16 * i, 16)
        lhs[left, :] = -block[48:, cot_half]
        rhs[left, :] = block[48:, :SIZE_K] * s_all
        right = pl.ds(64 + 48 * i, 48)
        lhs[right, :] = block[:48, cot_half] * s_half
        rhs[right, :] = block[:48, :SIZE_K]
        right = pl.ds(160 + 48 * i, 48)
        lhs[right, :] = -block[:48, half] * s_half
        rhs[right, :] = block[:48, SIZE_K:]
        right = pl.ds(32 + 48 * i, 48)
        lhs2[right, :] = block[:48, half] * inv_half
        rhs2[right, :] = block[:48, SIZE_K:]
    rows = ((0,), (0,))
    eye = lax.broadcasted_iota(jnp.int32, (HALF, HALF), 0) == (
        lax.broadcasted_iota(jnp.int32, (HALF, HALF), 1)
    )
    s_down = jnp.sum(jnp.where(eye, s_half, 0.0), axis=1, keepdims=True)
    spread = s_all * s_all - s_down * s_down
    diagonal = (lax.broadcasted_iota(jnp.int32, (HALF, SIZE_K), 0) + begin) == (
        lax.broadcasted_iota(jnp.int32, (HALF, SIZE_K), 1)
    )
    divided = jnp.where(diagonal, 0.0, 1.0 / jnp.where(diagonal, 1.0, spread))
    main = dot(lhs[...], rhs[...], rows, HIGHEST)
    out[...] = divided * main - dot(lhs2[...], rhs2[...], rows, HIGHEST)


def half_core(core_index, own, got, singular):
    vmem = pl.BlockSpec(memory_space=pltpu.VMEM)
    return pl.pallas_call(
        half_core_kernel,
        out_shape=jax.ShapeDtypeStruct((HALF, SIZE_K), jnp.float32),
        in_specs=[pl.BlockSpec(memory_space=pltpu.SMEM)] + [vmem] * 3,
        out_specs=vmem,
        scratch_shapes=[
            pltpu.VMEM((256, HALF), jnp.float32),
            pltpu.VMEM((256, SIZE_K), jnp.float32),
            pltpu.VMEM((128, HALF), jnp.float32),
            pltpu.VMEM((128, SIZE_K), jnp.float32),
        ],
        cost_estimate=pl.CostEstimate(
            flops=2 * 6 * 384 * HALF * SIZE_K, bytes_accessed=1 << 20, transcendentals=0
        ),
        compiler_params=pltpu.CompilerParams(vmem_limit_bytes=12 << 20),
        name="half_core",
    )(core_index.reshape(1), own, got, singular.reshape(1, -1))


def place_kernel(z, below, own, above, mid_below, mid_above, last_above, out):
    blocks = [own[...], above[...], mid_above[0], mid_above[1], last_above[...]]
    blocks = blocks + [mid_below[0], mid_below[1], below[...]]
    for i, block in enumerate(blocks):
        out[lax.rem(z[0] + i, 8)] = block


def merge_kernel(index, mine, theirs, out):
    out[:, index[0]] = mine[...]
    out[:, 1 - index[0]] = theirs[...]


def assemble(kernel, shape, index, *blocks):
    vmem = pl.BlockSpec(memory_space=pltpu.VMEM)
    return pl.pallas_call(
        kernel,
        out_shape=jax.ShapeDtypeStruct(shape, jnp.float32),
        in_specs=[pl.BlockSpec(memory_space=pltpu.SMEM)] + [vmem] * len(blocks),
        out_specs=vmem,
        cost_estimate=pl.CostEstimate(flops=0, bytes_accessed=2 << 20, transcendentals=0),
        compiler_params=pltpu.CompilerParams(vmem_limit_bytes=10 << 20),
    )(index.reshape(1), *blocks)


def local(left, left_cot, right, right_cot, singular, singular_cot):
    core_index = lax.axis_index("core")
    first = core_index == 0
    at_low = lax.axis_index("yl") == 0

    right_pair, left_pair, stacked = pack(left, left_cot, right, right_cot)
    rights = lax.all_gather(right_pair, ROW, axis=0, tiled=True)
    other = shift(left_pair, "yl", 2, 1)
    got = swap(stacked)
    mine = half_core(core_index, stacked, got, singular)
    pieces = lax.all_to_all(mine.reshape(16, 16, SIZE_K), OUTER, 0, 0)

    own = jnp.stack([jnp.where(at_low, left_pair, other), jnp.where(at_low, other, left_pair)])
    below, above = shift(own, Z, 8, 1), shift(own, Z, 8, -1)

    mid_below = shift(jnp.stack([below, own]), Z, 8, 2)
    mid_above = shift(jnp.stack([own, above]), Z, 8, -2)
    pieces = gather(jnp.sum(pieces, axis=0), INNER, 16)
    last_above = shift(mid_above[1], Z, 8, -1)
    blocks = (below, own, above, mid_below, mid_above, last_above)
    line = assemble(place_kernel, (8, 2, 16, 1024), lax.axis_index(Z), *blocks)
    line = line.reshape(16, 16, 1024)
    rows = jnp.sum(pieces, axis=0)
    own_half = gather(rows, OUTER, 16).reshape(HALF, SIZE_K)
    other_line = swap(line)
    lefts = assemble(
        merge_kernel, (16, 2, 16, 1024), core_index, line, other_line
    ).reshape(-1, 1024)
    other_half = swap(own_half)
    core = jnp.concatenate(
        [jnp.where(first, own_half, other_half), jnp.where(first, other_half, own_half)], axis=0
    ) + jnp.diag(singular_cot)

    inverse = (1.0 / singular)[None, :]
    factor = lefts[:, :SIZE_K]
    panel = dot(factor, core, ((1,), (0,)), HIGH) + lefts[:, SIZE_K:] * inverse
    both = jnp.concatenate([factor * inverse, panel], axis=1)
    return dot(both, rights, ((1,), (1,)), HIGH)


def solution(mesh):
    fine = Mesh(mesh.devices.reshape(SIZES), ALL)
    placed = (
        P(ROW + COL, None),
        P(ROW + COL, None),
        P(COL + ROW, None),
        P(COL + ROW, None),
        P(),
        P(),
    )
    return jax.shard_map(local, mesh=fine, in_specs=placed, out_specs=P(ROW, COL), check_vma=False)
```

```python
import jax
import jax.numpy as jnp
from jax import lax
from jax.experimental import pallas as pl
from jax.experimental.pallas import tpu as pltpu
from jax.sharding import Mesh
from jax.sharding import PartitionSpec as P

ROW = ("x", "yh")
COL = ("zh", "zl", "yl", "core")
ALL = ROW + COL
Z = ("zh", "zl")
OUTER = ("x", "zl", "yl")
SIZES = (4, 4, 4, 2, 2, 2)
SIZE_K = 512
HALF = 256
HIGHEST = lax.Precision.HIGHEST
HIGH = lax.Precision.HIGH
SWAP = [(0, 1), (1, 0)]


def dot(a, b, contract, precision):
    return lax.dot_general(
        a, b, (contract, ((), ())), precision=precision, preferred_element_type=jnp.float32
    )


def gather(block, axis, size):
    copies = jnp.broadcast_to(block[None], (size,) + block.shape)
    return lax.all_to_all(copies, axis, 0, 0)


def shift(block, axis, size, by):
    return lax.ppermute(block, axis, [(i, (i + by) % size) for i in range(size)])


def swap(block):
    return lax.ppermute(block, "core", SWAP)


def pack_kernel(left, left_cot, right, right_cot, right_pair, left_pair, stacked, held, sems):
    low, high = pl.ds(0, SIZE_K), pl.ds(SIZE_K, SIZE_K)
    top, bottom = pl.ds(0, 48), pl.ds(48, 16)

    def start(i, source, target):
        copy = pltpu.make_async_copy(source, target, sems.at[i])
        copy.start()
        return copy

    reads = [
        start(0, right_cot, held.at[top, low]),
        start(1, right, held.at[top, high]),
        start(2, left, held.at[bottom, low]),
        start(3, left_cot, held.at[bottom, high]),
    ]
    for copy in reads:
        copy.wait()
    writes = [
        start(4, held, stacked),
        start(5, held.at[top, :], right_pair),
        start(6, held.at[bottom, :], left_pair),
    ]
    for copy in writes:
        copy.wait()


def pack(left, left_cot, right, right_cot):
    shapes = ((48, 1024), (16, 1024), (64, 1024))
    hbm = pl.BlockSpec(memory_space=pl.ANY)
    return pl.pallas_call(
        pack_kernel,
        out_shape=[jax.ShapeDtypeStruct(s, jnp.float32) for s in shapes],
        in_specs=[hbm] * 4,
        out_specs=[hbm] * 3,
        scratch_shapes=[
            pltpu.VMEM((64, 1024), jnp.float32),
            pltpu.SemaphoreType.DMA((7,)),
        ],
        cost_estimate=pl.CostEstimate(flops=0, bytes_accessed=1 << 20, transcendentals=0),
        name="pack",
    )(left, left_cot, right, right_cot)


def half_core_kernel(core_index, own, got, s_row, out, lhs, rhs, lhs2, rhs2):
    begin = pl.multiple_of(core_index[0] * HALF, HALF)
    half = pl.ds(begin, HALF)
    cot_half = pl.ds(pl.multiple_of(begin + SIZE_K, HALF), HALF)
    s_all = s_row[...]
    s_half = s_row[:, half]
    inv_all = 1.0 / s_all
    inv_half = 1.0 / s_half
    for i, block in enumerate((own, got)):
        left = pl.ds(16 * i, 16)
        lhs[left, :] = block[48:, half]
        rhs[left, :] = block[48:, SIZE_K:] * s_all
        lhs2[left, :] = block[48:, half]
        rhs2[left, :] = block[48:, SIZE_K:] * inv_all
        left = pl.ds(32 + 16 * i, 16)
        lhs[left, :] = -block[48:, cot_half]
        rhs[left, :] = block[48:, :SIZE_K] * s_all
        right = pl.ds(64 + 48 * i, 48)
        lhs[right, :] = block[:48, cot_half] * s_half
        rhs[right, :] = block[:48, :SIZE_K]
        right = pl.ds(160 + 48 * i, 48)
        lhs[right, :] = -block[:48, half] * s_half
        rhs[right, :] = block[:48, SIZE_K:]
        right = pl.ds(32 + 48 * i, 48)
        lhs2[right, :] = block[:48, half] * inv_half
        rhs2[right, :] = block[:48, SIZE_K:]
    rows = ((0,), (0,))
    eye = lax.broadcasted_iota(jnp.int32, (HALF, HALF), 0) == (
        lax.broadcasted_iota(jnp.int32, (HALF, HALF), 1)
    )
    s_down = jnp.sum(jnp.where(eye, s_half, 0.0), axis=1, keepdims=True)
    spread = s_all * s_all - s_down * s_down
    diagonal = (lax.broadcasted_iota(jnp.int32, (HALF, SIZE_K), 0) + begin) == (
        lax.broadcasted_iota(jnp.int32, (HALF, SIZE_K), 1)
    )
    divided = jnp.where(diagonal, 0.0, 1.0 / jnp.where(diagonal, 1.0, spread))
    main = dot(lhs[...], rhs[...], rows, HIGHEST)
    out[...] = divided * main - dot(lhs2[...], rhs2[...], rows, HIGHEST)


def half_core(core_index, own, got, singular):
    vmem = pl.BlockSpec(memory_space=pltpu.VMEM)
    return pl.pallas_call(
        half_core_kernel,
        out_shape=jax.ShapeDtypeStruct((HALF, SIZE_K), jnp.float32),
        in_specs=[pl.BlockSpec(memory_space=pltpu.SMEM)] + [vmem] * 3,
        out_specs=vmem,
        scratch_shapes=[
            pltpu.VMEM((256, HALF), jnp.float32),
            pltpu.VMEM((256, SIZE_K), jnp.float32),
            pltpu.VMEM((128, HALF), jnp.float32),
            pltpu.VMEM((128, SIZE_K), jnp.float32),
        ],
        cost_estimate=pl.CostEstimate(
            flops=2 * 6 * 384 * HALF * SIZE_K, bytes_accessed=1 << 20, transcendentals=0
        ),
        compiler_params=pltpu.CompilerParams(vmem_limit_bytes=12 << 20),
        name="half_core",
    )(core_index.reshape(1), own, got, singular.reshape(1, -1))


def place_kernel(z, below, own, above, mid_below, mid_above, last_above, out):
    blocks = [own[...], above[...], mid_above[0], mid_above[1], last_above[...]]
    blocks = blocks + [mid_below[0], mid_below[1], below[...]]
    for i, block in enumerate(blocks):
        out[lax.rem(z[0] + i, 8)] = block


def merge_kernel(index, mine, theirs, out):
    out[:, index[0]] = mine[...]
    out[:, 1 - index[0]] = theirs[...]


def assemble(kernel, shape, index, *blocks):
    vmem = pl.BlockSpec(memory_space=pltpu.VMEM)
    return pl.pallas_call(
        kernel,
        out_shape=jax.ShapeDtypeStruct(shape, jnp.float32),
        in_specs=[pl.BlockSpec(memory_space=pltpu.SMEM)] + [vmem] * len(blocks),
        out_specs=vmem,
        cost_estimate=pl.CostEstimate(flops=0, bytes_accessed=2 << 20, transcendentals=0),
        compiler_params=pltpu.CompilerParams(vmem_limit_bytes=10 << 20),
    )(index.reshape(1), *blocks)


def local(left, left_cot, right, right_cot, singular, singular_cot):
    core_index = lax.axis_index("core")
    at_low = lax.axis_index("yl") == 0

    right_pair, left_pair, stacked = pack(left, left_cot, right, right_cot)
    rights = lax.all_gather(right_pair, ROW, axis=0, tiled=True)
    other = shift(left_pair, "yl", 2, 1)
    got = swap(stacked)
    mine = half_core(core_index, stacked, got, singular)
    pieces = lax.all_to_all(mine.reshape(16, 16, SIZE_K), OUTER, 0, 0)

    own = jnp.stack([jnp.where(at_low, left_pair, other), jnp.where(at_low, other, left_pair)])
    below, above = shift(own, Z, 8, 1), shift(own, Z, 8, -1)

    mid_below = shift(jnp.stack([below, own]), Z, 8, 2)
    mid_above = shift(jnp.stack([own, above]), Z, 8, -2)
    pieces = gather(jnp.sum(pieces, axis=0), "yh", 4)
    pieces = gather(jnp.sum(pieces, axis=0), "zh", 4)
    last_above = shift(mid_above[1], Z, 8, -1)
    blocks = (below, own, above, mid_below, mid_above, last_above)
    line = assemble(place_kernel, (8, 2, 16, 1024), lax.axis_index(Z), *blocks)
    line = line.reshape(16, 16, 1024)
    rows = jnp.sum(pieces, axis=0)
    own_half = gather(rows, OUTER, 16).reshape(HALF, SIZE_K)
    other_line = swap(line)
    lefts = assemble(
        merge_kernel, (16, 2, 16, 1024), core_index, line, other_line
    ).reshape(-1, 1024)
    other_half = swap(own_half)
    halves = (own_half[None], other_half[None])
    core = assemble(merge_kernel, (1, 2, HALF, SIZE_K), core_index, *halves)
    core = core.reshape(SIZE_K, SIZE_K)

    inverse = (1.0 / singular)[None, :]
    factor = lefts[:, :SIZE_K]
    panel = dot(factor, core, ((1,), (0,)), HIGH) + factor * singular_cot[None, :]
    panel = panel + lefts[:, SIZE_K:] * inverse
    both = jnp.concatenate([factor * inverse, panel], axis=1)
    return dot(both, rights, ((1,), (1,)), HIGH)


def solution(mesh):
    fine = Mesh(mesh.devices.reshape(SIZES), ALL)
    placed = (
        P(ROW + COL, None),
        P(ROW + COL, None),
        P(COL + ROW, None),
        P(COL + ROW, None),
        P(),
        P(),
    )
    return jax.shard_map(local, mesh=fine, in_specs=placed, out_specs=P(ROW, COL), check_vma=False)
```

```python
import jax
import jax.numpy as jnp
from jax import lax
from jax.experimental import pallas as pl
from jax.experimental.pallas import tpu as pltpu
from jax.sharding import Mesh
from jax.sharding import PartitionSpec as P

ROW = ("x", "yh")
COL = ("zh", "zl", "yl", "core")
ALL = ROW + COL
Z = ("zh", "zl")
OUTER = ("x", "zl", "yl")
SIZES = (4, 4, 4, 2, 2, 2)
SIZE_K = 512
HALF = 256
HIGHEST = lax.Precision.HIGHEST
HIGH = lax.Precision.HIGH
SWAP = [(0, 1), (1, 0)]


def dot(a, b, contract, precision):
    return lax.dot_general(
        a, b, (contract, ((), ())), precision=precision, preferred_element_type=jnp.float32
    )


def gather(block, axis, size):
    copies = jnp.broadcast_to(block[None], (size,) + block.shape)
    return lax.all_to_all(copies, axis, 0, 0)


def swap(block):
    return lax.ppermute(block, "core", SWAP)


def pack_kernel(left, left_cot, right, right_cot, right_pair, left_pair, stacked, held, sems):
    low, high = pl.ds(0, SIZE_K), pl.ds(SIZE_K, SIZE_K)
    top, bottom = pl.ds(0, 48), pl.ds(48, 16)

    def start(i, source, target):
        copy = pltpu.make_async_copy(source, target, sems.at[i])
        copy.start()
        return copy

    reads = [
        start(0, right_cot, held.at[top, low]),
        start(1, right, held.at[top, high]),
        start(2, left, held.at[bottom, low]),
        start(3, left_cot, held.at[bottom, high]),
    ]
    for copy in reads:
        copy.wait()
    writes = [
        start(4, held, stacked),
        start(5, held.at[top, :], right_pair),
        start(6, held.at[bottom, :], left_pair),
    ]
    for copy in writes:
        copy.wait()


def pack(left, left_cot, right, right_cot):
    shapes = ((48, 1024), (16, 1024), (64, 1024))
    hbm = pl.BlockSpec(memory_space=pl.ANY)
    return pl.pallas_call(
        pack_kernel,
        out_shape=[jax.ShapeDtypeStruct(s, jnp.float32) for s in shapes],
        in_specs=[hbm] * 4,
        out_specs=[hbm] * 3,
        scratch_shapes=[
            pltpu.VMEM((64, 1024), jnp.float32),
            pltpu.SemaphoreType.DMA((7,)),
        ],
        cost_estimate=pl.CostEstimate(flops=0, bytes_accessed=1 << 20, transcendentals=0),
        name="pack",
    )(left, left_cot, right, right_cot)


def half_core_kernel(core_index, own, got, s_row, out, lhs, rhs, lhs2, rhs2):
    begin = pl.multiple_of(core_index[0] * HALF, HALF)
    half = pl.ds(begin, HALF)
    cot_half = pl.ds(pl.multiple_of(begin + SIZE_K, HALF), HALF)
    s_all = s_row[...]
    s_half = s_row[:, half]
    inv_all = 1.0 / s_all
    inv_half = 1.0 / s_half
    for i, block in enumerate((own, got)):
        left = pl.ds(16 * i, 16)
        lhs[left, :] = block[48:, half]
        rhs[left, :] = block[48:, SIZE_K:] * s_all
        lhs2[left, :] = block[48:, half]
        rhs2[left, :] = block[48:, SIZE_K:] * inv_all
        left = pl.ds(32 + 16 * i, 16)
        lhs[left, :] = -block[48:, cot_half]
        rhs[left, :] = block[48:, :SIZE_K] * s_all
        right = pl.ds(64 + 48 * i, 48)
        lhs[right, :] = block[:48, cot_half] * s_half
        rhs[right, :] = block[:48, :SIZE_K]
        right = pl.ds(160 + 48 * i, 48)
        lhs[right, :] = -block[:48, half] * s_half
        rhs[right, :] = block[:48, SIZE_K:]
        right = pl.ds(32 + 48 * i, 48)
        lhs2[right, :] = block[:48, half] * inv_half
        rhs2[right, :] = block[:48, SIZE_K:]
    rows = ((0,), (0,))
    eye = lax.broadcasted_iota(jnp.int32, (HALF, HALF), 0) == (
        lax.broadcasted_iota(jnp.int32, (HALF, HALF), 1)
    )
    s_down = jnp.sum(jnp.where(eye, s_half, 0.0), axis=1, keepdims=True)
    spread = s_all * s_all - s_down * s_down
    diagonal = (lax.broadcasted_iota(jnp.int32, (HALF, SIZE_K), 0) + begin) == (
        lax.broadcasted_iota(jnp.int32, (HALF, SIZE_K), 1)
    )
    divided = jnp.where(diagonal, 0.0, 1.0 / jnp.where(diagonal, 1.0, spread))
    main = dot(lhs[...], rhs[...], rows, HIGHEST)
    out[...] = divided * main - dot(lhs2[...], rhs2[...], rows, HIGHEST)


def half_core(core_index, own, got, singular):
    vmem = pl.BlockSpec(memory_space=pltpu.VMEM)
    return pl.pallas_call(
        half_core_kernel,
        out_shape=jax.ShapeDtypeStruct((HALF, SIZE_K), jnp.float32),
        in_specs=[pl.BlockSpec(memory_space=pltpu.SMEM)] + [vmem] * 3,
        out_specs=vmem,
        scratch_shapes=[
            pltpu.VMEM((256, HALF), jnp.float32),
            pltpu.VMEM((256, SIZE_K), jnp.float32),
            pltpu.VMEM((128, HALF), jnp.float32),
            pltpu.VMEM((128, SIZE_K), jnp.float32),
        ],
        cost_estimate=pl.CostEstimate(
            flops=2 * 6 * 384 * HALF * SIZE_K, bytes_accessed=1 << 20, transcendentals=0
        ),
        compiler_params=pltpu.CompilerParams(vmem_limit_bytes=12 << 20),
        name="half_core",
    )(core_index.reshape(1), own, got, singular.reshape(1, -1))


def merge_kernel(index, mine, theirs, out):
    out[:, index[0]] = mine[...]
    out[:, 1 - index[0]] = theirs[...]


def assemble(kernel, shape, index, *blocks):
    vmem = pl.BlockSpec(memory_space=pltpu.VMEM)
    return pl.pallas_call(
        kernel,
        out_shape=jax.ShapeDtypeStruct(shape, jnp.float32),
        in_specs=[pl.BlockSpec(memory_space=pltpu.SMEM)] + [vmem] * len(blocks),
        out_specs=vmem,
        cost_estimate=pl.CostEstimate(flops=0, bytes_accessed=2 << 20, transcendentals=0),
        compiler_params=pltpu.CompilerParams(vmem_limit_bytes=10 << 20),
    )(index.reshape(1), *blocks)


def local(left, left_cot, right, right_cot, singular, singular_cot):
    core_index = lax.axis_index("core")

    right_pair, left_pair, stacked = pack(left, left_cot, right, right_cot)
    rights = lax.all_gather(right_pair, ROW, axis=0, tiled=True)
    line = gather(left_pair, Z, 8)
    got = swap(stacked)
    mine = half_core(core_index, stacked, got, singular)
    pieces = lax.all_to_all(mine.reshape(16, 16, SIZE_K), OUTER, 0, 0)
    other_line = lax.ppermute(line, "yl", SWAP)
    pieces = gather(jnp.sum(pieces, axis=0), "zh", 4)
    pieces = gather(jnp.sum(pieces, axis=0), "yh", 4)
    plane = assemble(
        merge_kernel, (8, 2, 16, 1024), lax.axis_index("yl"), line, other_line
    ).reshape(16, 16, 1024)
    other_plane = swap(plane)
    rows = jnp.sum(pieces, axis=0)
    own_half = gather(rows, OUTER, 16).reshape(HALF, SIZE_K)
    lefts = assemble(
        merge_kernel, (16, 2, 16, 1024), core_index, plane, other_plane
    ).reshape(-1, 1024)
    other_half = swap(own_half)
    halves = (own_half[None], other_half[None])
    core = assemble(merge_kernel, (1, 2, HALF, SIZE_K), core_index, *halves)
    core = core.reshape(SIZE_K, SIZE_K)

    inverse = (1.0 / singular)[None, :]
    factor = lefts[:, :SIZE_K]
    panel = dot(factor, core, ((1,), (0,)), HIGH) + factor * singular_cot[None, :]
    panel = panel + lefts[:, SIZE_K:] * inverse
    both = jnp.concatenate([factor * inverse, panel], axis=1)
    return dot(both, rights, ((1,), (1,)), HIGH)


def solution(mesh):
    fine = Mesh(mesh.devices.reshape(SIZES), ALL)
    placed = (
        P(ROW + COL, None),
        P(ROW + COL, None),
        P(COL + ROW, None),
        P(COL + ROW, None),
        P(),
        P(),
    )
    return jax.shard_map(local, mesh=fine, in_specs=placed, out_specs=P(ROW, COL), check_vma=False)
```

```python
import jax
import jax.numpy as jnp
from jax import lax
from jax.experimental import pallas as pl
from jax.experimental.pallas import tpu as pltpu
from jax.sharding import Mesh
from jax.sharding import PartitionSpec as P

ROW = ("x", "yh")
COL = ("zh", "zl", "yl", "core")
ALL = ROW + COL
Z = ("zh", "zl")
OUTER = ("x", "zl", "yl")
INNER = ("yh", "zh")
SIZES = (4, 4, 4, 2, 2, 2)
SIZE_K = 512
HALF = 256
PRODUCT_LIMIT = 50 << 20
HIGHEST = lax.Precision.HIGHEST
SWAP = [(0, 1), (1, 0)]


def dot(a, b, contract, precision):
    return lax.dot_general(
        a, b, (contract, ((), ())), precision=precision, preferred_element_type=jnp.float32
    )


def gather(block, axis, size):
    copies = jnp.broadcast_to(block[None], (size,) + block.shape)
    return lax.all_to_all(copies, axis, 0, 0)


def shift(block, axis, size, by):
    return lax.ppermute(block, axis, [(i, (i + by) % size) for i in range(size)])


def swap(block):
    return lax.ppermute(block, "core", SWAP)


def pack_kernel(left, left_cot, right, right_cot, right_pair, left_pair, stacked, held, sems):
    low, high = pl.ds(0, SIZE_K), pl.ds(SIZE_K, SIZE_K)
    top, bottom = pl.ds(0, 48), pl.ds(48, 16)

    def start(i, source, target):
        copy = pltpu.make_async_copy(source, target, sems.at[i])
        copy.start()
        return copy

    reads = [
        start(0, right_cot, held.at[top, low]),
        start(1, right, held.at[top, high]),
        start(2, left, held.at[bottom, low]),
        start(3, left_cot, held.at[bottom, high]),
    ]
    for copy in reads:
        copy.wait()
    writes = [
        start(4, held, stacked),
        start(5, held.at[top, :], right_pair),
        start(6, held.at[bottom, :], left_pair),
    ]
    for copy in writes:
        copy.wait()


def pack(left, left_cot, right, right_cot):
    shapes = ((48, 1024), (16, 1024), (64, 1024))
    hbm = pl.BlockSpec(memory_space=pl.ANY)
    return pl.pallas_call(
        pack_kernel,
        out_shape=[jax.ShapeDtypeStruct(s, jnp.float32) for s in shapes],
        in_specs=[hbm] * 4,
        out_specs=[hbm] * 3,
        scratch_shapes=[
            pltpu.VMEM((64, 1024), jnp.float32),
            pltpu.SemaphoreType.DMA((7,)),
        ],
        cost_estimate=pl.CostEstimate(flops=0, bytes_accessed=1 << 20, transcendentals=0),
        name="pack",
    )(left, left_cot, right, right_cot)


def half_core_kernel(core_index, own, got, s_row, out, lhs, rhs, lhs2, rhs2):
    begin = pl.multiple_of(core_index[0] * HALF, HALF)
    half = pl.ds(begin, HALF)
    cot_half = pl.ds(pl.multiple_of(begin + SIZE_K, HALF), HALF)
    s_all = s_row[...]
    s_half = s_row[:, half]
    inv_all = 1.0 / s_all
    inv_half = 1.0 / s_half
    for i, block in enumerate((own, got)):
        left = pl.ds(16 * i, 16)
        lhs[left, :] = block[48:, half]
        rhs[left, :] = block[48:, SIZE_K:] * s_all
        lhs2[left, :] = block[48:, half]
        rhs2[left, :] = block[48:, SIZE_K:] * inv_all
        left = pl.ds(32 + 16 * i, 16)
        lhs[left, :] = -block[48:, cot_half]
        rhs[left, :] = block[48:, :SIZE_K] * s_all
        right = pl.ds(64 + 48 * i, 48)
        lhs[right, :] = block[:48, cot_half] * s_half
        rhs[right, :] = block[:48, :SIZE_K]
        right = pl.ds(160 + 48 * i, 48)
        lhs[right, :] = -block[:48, half] * s_half
        rhs[right, :] = block[:48, SIZE_K:]
        right = pl.ds(32 + 48 * i, 48)
        lhs2[right, :] = block[:48, half] * inv_half
        rhs2[right, :] = block[:48, SIZE_K:]
    rows = ((0,), (0,))
    eye = lax.broadcasted_iota(jnp.int32, (HALF, HALF), 0) == (
        lax.broadcasted_iota(jnp.int32, (HALF, HALF), 1)
    )
    s_down = jnp.sum(jnp.where(eye, s_half, 0.0), axis=1, keepdims=True)
    spread = s_all * s_all - s_down * s_down
    diagonal = (lax.broadcasted_iota(jnp.int32, (HALF, SIZE_K), 0) + begin) == (
        lax.broadcasted_iota(jnp.int32, (HALF, SIZE_K), 1)
    )
    divided = jnp.where(diagonal, 0.0, 1.0 / jnp.where(diagonal, 1.0, spread))
    main = dot(lhs[...], rhs[...], rows, HIGHEST)
    out[...] = divided * main - dot(lhs2[...], rhs2[...], rows, HIGHEST)


def half_core(core_index, own, got, singular):
    vmem = pl.BlockSpec(memory_space=pltpu.VMEM)
    return pl.pallas_call(
        half_core_kernel,
        out_shape=jax.ShapeDtypeStruct((HALF, SIZE_K), jnp.float32),
        in_specs=[pl.BlockSpec(memory_space=pltpu.SMEM)] + [vmem] * 3,
        out_specs=vmem,
        scratch_shapes=[
            pltpu.VMEM((256, HALF), jnp.float32),
            pltpu.VMEM((256, SIZE_K), jnp.float32),
            pltpu.VMEM((128, HALF), jnp.float32),
            pltpu.VMEM((128, SIZE_K), jnp.float32),
        ],
        cost_estimate=pl.CostEstimate(
            flops=2 * 6 * 384 * HALF * SIZE_K, bytes_accessed=1 << 20, transcendentals=0
        ),
        compiler_params=pltpu.CompilerParams(vmem_limit_bytes=12 << 20),
        name="half_core",
    )(core_index.reshape(1), own, got, singular.reshape(1, -1))


def place_kernel(z, below, own, above, mid_below, mid_above, last_above, out):
    blocks = [own[...], above[...], mid_above[0], mid_above[1], last_above[...]]
    blocks = blocks + [mid_below[0], mid_below[1], below[...]]
    for i, block in enumerate(blocks):
        out[lax.rem(z[0] + i, 8)] = block


def merge_kernel(index, mine, theirs, out):
    out[:, index[0]] = mine[...]
    out[:, 1 - index[0]] = theirs[...]


def assemble(kernel, shape, index, *blocks):
    vmem = pl.BlockSpec(memory_space=pltpu.VMEM)
    return pl.pallas_call(
        kernel,
        out_shape=jax.ShapeDtypeStruct(shape, jnp.float32),
        in_specs=[pl.BlockSpec(memory_space=pltpu.SMEM)] + [vmem] * len(blocks),
        out_specs=vmem,
        cost_estimate=pl.CostEstimate(flops=0, bytes_accessed=2 << 20, transcendentals=0),
        compiler_params=pltpu.CompilerParams(vmem_limit_bytes=10 << 20),
    )(index.reshape(1), *blocks)


def split(a):
    high = a.astype(jnp.bfloat16)
    return high, (a - high.astype(jnp.float32)).astype(jnp.bfloat16)


def dot3(a, b, contract):
    a_high, a_low = a
    b_high, b_low = b
    small = dot(a_high, b_low, contract, None) + dot(a_low, b_high, contract, None)
    return dot(a_high, b_high, contract, None) + small


def panel_kernel(core_index, lefts, own_half, other_half, s_row, cot_row, high, low, core):
    first = pl.ds(pl.multiple_of(core_index[0] * HALF, HALF), HALF)
    second = pl.ds(pl.multiple_of((1 - core_index[0]) * HALF, HALF), HALF)
    core[first, :] = own_half[...]
    core[second, :] = other_half[...]
    inverse = 1.0 / s_row[...]
    factor = lefts[:, :SIZE_K]
    high[:, :SIZE_K], low[:, :SIZE_K] = split(factor * inverse)
    whole = dot3(split(factor), split(core[...]), ((1,), (0,)))
    whole = whole + factor * cot_row[...] + lefts[:, SIZE_K:] * inverse
    high[:, SIZE_K:], low[:, SIZE_K:] = split(whole)


def panel(core_index, lefts, own_half, other_half, singular, singular_cot):
    vmem = pl.BlockSpec(memory_space=pltpu.VMEM)
    return pl.pallas_call(
        panel_kernel,
        out_shape=[jax.ShapeDtypeStruct((512, 2 * SIZE_K), jnp.bfloat16)] * 2,
        in_specs=[pl.BlockSpec(memory_space=pltpu.SMEM)] + [vmem] * 5,
        out_specs=[vmem] * 2,
        scratch_shapes=[pltpu.VMEM((SIZE_K, SIZE_K), jnp.float32)],
        cost_estimate=pl.CostEstimate(
            flops=6 * 512 * SIZE_K * SIZE_K, bytes_accessed=5 << 20, transcendentals=0
        ),
        compiler_params=pltpu.CompilerParams(vmem_limit_bytes=24 << 20),
        name="panel",
    )(
        core_index.reshape(1),
        lefts,
        own_half,
        other_half,
        singular.reshape(1, -1),
        singular_cot.reshape(1, -1),
    )


def product_kernel(high, low, rights, out):
    out[...] = dot3((high[...], low[...]), split(rights[...]), ((1,), (1,)))


def product(high, low, rights):
    width = 2 * SIZE_K
    step = 256
    whole = pl.BlockSpec((512, width), lambda i: (0, 0))
    return pl.pallas_call(
        product_kernel,
        out_shape=jax.ShapeDtypeStruct((512, 768), jnp.float32),
        grid=(768 // step,),
        in_specs=[whole, whole, pl.BlockSpec((step, width), lambda i: (i, 0))],
        out_specs=pl.BlockSpec((512, step), lambda i: (0, i)),
        cost_estimate=pl.CostEstimate(
            flops=6 * 512 * 768 * width, bytes_accessed=7 << 20, transcendentals=0
        ),
        compiler_params=pltpu.CompilerParams(vmem_limit_bytes=PRODUCT_LIMIT),
        name="product",
    )(high, low, rights)


def local(left, left_cot, right, right_cot, singular, singular_cot):
    core_index = lax.axis_index("core")
    at_low = lax.axis_index("yl") == 0

    right_pair, left_pair, stacked = pack(left, left_cot, right, right_cot)
    rights = lax.all_gather(right_pair, ROW, axis=0, tiled=True)
    other = shift(left_pair, "yl", 2, 1)
    got = swap(stacked)
    mine = half_core(core_index, stacked, got, singular)
    pieces = lax.all_to_all(mine.reshape(16, 16, SIZE_K), OUTER, 0, 0)

    own = jnp.stack([jnp.where(at_low, left_pair, other), jnp.where(at_low, other, left_pair)])
    below, above = shift(own, Z, 8, 1), shift(own, Z, 8, -1)

    mid_below = shift(jnp.stack([below, own]), Z, 8, 2)
    mid_above = shift(jnp.stack([own, above]), Z, 8, -2)
    pieces = gather(jnp.sum(pieces, axis=0), INNER, 16)
    last_above = shift(mid_above[1], Z, 8, -1)
    blocks = (below, own, above, mid_below, mid_above, last_above)
    line = assemble(place_kernel, (8, 2, 16, 1024), lax.axis_index(Z), *blocks)
    line = line.reshape(16, 16, 1024)
    rows = jnp.sum(pieces, axis=0)
    own_half = gather(rows, OUTER, 16).reshape(HALF, SIZE_K)
    other_line = swap(line)
    lefts = assemble(
        merge_kernel, (16, 2, 16, 1024), core_index, line, other_line
    ).reshape(-1, 1024)
    other_half = swap(own_half)
    high, low = panel(core_index, lefts, own_half, other_half, singular, singular_cot)
    return product(high, low, rights)


def solution(mesh):
    fine = Mesh(mesh.devices.reshape(SIZES), ALL)
    placed = (
        P(ROW + COL, None),
        P(ROW + COL, None),
        P(COL + ROW, None),
        P(COL + ROW, None),
        P(),
        P(),
    )
    return jax.shard_map(local, mesh=fine, in_specs=placed, out_specs=P(ROW, COL), check_vma=False)
```

```python
import jax
import jax.numpy as jnp
from jax import lax
from jax.experimental import pallas as pl
from jax.experimental.pallas import tpu as pltpu
from jax.sharding import Mesh
from jax.sharding import PartitionSpec as P

ROW = ("x", "yh")
COL = ("zh", "zl", "yl", "core")
ALL = ROW + COL
Z = ("zh", "zl")
OUTER = ("x", "zl", "yl")
SIZES = (4, 4, 4, 2, 2, 2)
SIZE_K = 512
HALF = 256
PRODUCT_LIMIT = 50 << 20
HIGHEST = lax.Precision.HIGHEST
SWAP = [(0, 1), (1, 0)]


def dot(a, b, contract, precision):
    return lax.dot_general(
        a, b, (contract, ((), ())), precision=precision, preferred_element_type=jnp.float32
    )


def gather(block, axis, size):
    copies = jnp.broadcast_to(block[None], (size,) + block.shape)
    return lax.all_to_all(copies, axis, 0, 0)


def shift(block, axis, size, by):
    return lax.ppermute(block, axis, [(i, (i + by) % size) for i in range(size)])


def swap(block):
    return lax.ppermute(block, "core", SWAP)


def pack_kernel(left, left_cot, right, right_cot, right_pair, left_pair, stacked, held, sems):
    low, high = pl.ds(0, SIZE_K), pl.ds(SIZE_K, SIZE_K)
    top, bottom = pl.ds(0, 48), pl.ds(48, 16)

    def start(i, source, target):
        copy = pltpu.make_async_copy(source, target, sems.at[i])
        copy.start()
        return copy

    reads = [
        start(0, right_cot, held.at[top, low]),
        start(1, right, held.at[top, high]),
        start(2, left, held.at[bottom, low]),
        start(3, left_cot, held.at[bottom, high]),
    ]
    for copy in reads:
        copy.wait()
    writes = [
        start(4, held, stacked),
        start(5, held.at[top, :], right_pair),
        start(6, held.at[bottom, :], left_pair),
    ]
    for copy in writes:
        copy.wait()


def pack(left, left_cot, right, right_cot):
    shapes = ((48, 1024), (16, 1024), (64, 1024))
    hbm = pl.BlockSpec(memory_space=pl.ANY)
    return pl.pallas_call(
        pack_kernel,
        out_shape=[jax.ShapeDtypeStruct(s, jnp.float32) for s in shapes],
        in_specs=[hbm] * 4,
        out_specs=[hbm] * 3,
        scratch_shapes=[
            pltpu.VMEM((64, 1024), jnp.float32),
            pltpu.SemaphoreType.DMA((7,)),
        ],
        cost_estimate=pl.CostEstimate(flops=0, bytes_accessed=1 << 20, transcendentals=0),
        name="pack",
    )(left, left_cot, right, right_cot)


def half_core_kernel(core_index, own, got, s_row, out, lhs, rhs, lhs2, rhs2):
    begin = pl.multiple_of(core_index[0] * HALF, HALF)
    half = pl.ds(begin, HALF)
    cot_half = pl.ds(pl.multiple_of(begin + SIZE_K, HALF), HALF)
    s_all = s_row[...]
    s_half = s_row[:, half]
    inv_all = 1.0 / s_all
    inv_half = 1.0 / s_half
    for i, block in enumerate((own, got)):
        left = pl.ds(16 * i, 16)
        lhs[left, :] = block[48:, half]
        rhs[left, :] = block[48:, SIZE_K:] * s_all
        lhs2[left, :] = block[48:, half]
        rhs2[left, :] = block[48:, SIZE_K:] * inv_all
        left = pl.ds(32 + 16 * i, 16)
        lhs[left, :] = -block[48:, cot_half]
        rhs[left, :] = block[48:, :SIZE_K] * s_all
        right = pl.ds(64 + 48 * i, 48)
        lhs[right, :] = block[:48, cot_half] * s_half
        rhs[right, :] = block[:48, :SIZE_K]
        right = pl.ds(160 + 48 * i, 48)
        lhs[right, :] = -block[:48, half] * s_half
        rhs[right, :] = block[:48, SIZE_K:]
        right = pl.ds(32 + 48 * i, 48)
        lhs2[right, :] = block[:48, half] * inv_half
        rhs2[right, :] = block[:48, SIZE_K:]
    rows = ((0,), (0,))
    eye = lax.broadcasted_iota(jnp.int32, (HALF, HALF), 0) == (
        lax.broadcasted_iota(jnp.int32, (HALF, HALF), 1)
    )
    s_down = jnp.sum(jnp.where(eye, s_half, 0.0), axis=1, keepdims=True)
    spread = s_all * s_all - s_down * s_down
    diagonal = (lax.broadcasted_iota(jnp.int32, (HALF, SIZE_K), 0) + begin) == (
        lax.broadcasted_iota(jnp.int32, (HALF, SIZE_K), 1)
    )
    divided = jnp.where(diagonal, 0.0, 1.0 / jnp.where(diagonal, 1.0, spread))
    main = dot(lhs[...], rhs[...], rows, HIGHEST)
    out[...] = divided * main - dot(lhs2[...], rhs2[...], rows, HIGHEST)


def half_core(core_index, own, got, singular):
    vmem = pl.BlockSpec(memory_space=pltpu.VMEM)
    return pl.pallas_call(
        half_core_kernel,
        out_shape=jax.ShapeDtypeStruct((HALF, SIZE_K), jnp.float32),
        in_specs=[pl.BlockSpec(memory_space=pltpu.SMEM)] + [vmem] * 3,
        out_specs=vmem,
        scratch_shapes=[
            pltpu.VMEM((256, HALF), jnp.float32),
            pltpu.VMEM((256, SIZE_K), jnp.float32),
            pltpu.VMEM((128, HALF), jnp.float32),
            pltpu.VMEM((128, SIZE_K), jnp.float32),
        ],
        cost_estimate=pl.CostEstimate(
            flops=2 * 6 * 384 * HALF * SIZE_K, bytes_accessed=1 << 20, transcendentals=0
        ),
        compiler_params=pltpu.CompilerParams(vmem_limit_bytes=12 << 20),
        name="half_core",
    )(core_index.reshape(1), own, got, singular.reshape(1, -1))


def place_kernel(z, below, own, mid_below, mid_above, last_above, out):
    blocks = [own[...], mid_above[0], mid_above[1], last_above[0], last_above[1]]
    blocks = blocks + [mid_below[0], mid_below[1], below[...]]
    for i, block in enumerate(blocks):
        out[lax.rem(z[0] + i, 8)] = block


def merge_kernel(index, mine, theirs, out):
    out[:, index[0]] = mine[...]
    out[:, 1 - index[0]] = theirs[...]


def assemble(kernel, shape, index, *blocks):
    vmem = pl.BlockSpec(memory_space=pltpu.VMEM)
    return pl.pallas_call(
        kernel,
        out_shape=jax.ShapeDtypeStruct(shape, jnp.float32),
        in_specs=[pl.BlockSpec(memory_space=pltpu.SMEM)] + [vmem] * len(blocks),
        out_specs=vmem,
        cost_estimate=pl.CostEstimate(flops=0, bytes_accessed=2 << 20, transcendentals=0),
        compiler_params=pltpu.CompilerParams(vmem_limit_bytes=10 << 20),
    )(index.reshape(1), *blocks)


def split(a):
    high = a.astype(jnp.bfloat16)
    return high, (a - high.astype(jnp.float32)).astype(jnp.bfloat16)


def dot3(a, b, contract):
    a_high, a_low = a
    b_high, b_low = b
    small = dot(a_high, b_low, contract, None) + dot(a_low, b_high, contract, None)
    return dot(a_high, b_high, contract, None) + small


def panel_kernel(core_index, lefts, own_half, other_half, s_row, cot_row, high, low, core):
    first = pl.ds(pl.multiple_of(core_index[0] * HALF, HALF), HALF)
    second = pl.ds(pl.multiple_of((1 - core_index[0]) * HALF, HALF), HALF)
    core[first, :] = own_half[...]
    core[second, :] = other_half[...]
    inverse = 1.0 / s_row[...]
    factor = lefts[:, :SIZE_K]
    high[:, :SIZE_K], low[:, :SIZE_K] = split(factor * inverse)
    whole = dot3(split(factor), split(core[...]), ((1,), (0,)))
    whole = whole + factor * cot_row[...] + lefts[:, SIZE_K:] * inverse
    high[:, SIZE_K:], low[:, SIZE_K:] = split(whole)


def panel(core_index, lefts, own_half, other_half, singular, singular_cot):
    vmem = pl.BlockSpec(memory_space=pltpu.VMEM)
    return pl.pallas_call(
        panel_kernel,
        out_shape=[jax.ShapeDtypeStruct((512, 2 * SIZE_K), jnp.bfloat16)] * 2,
        in_specs=[pl.BlockSpec(memory_space=pltpu.SMEM)] + [vmem] * 5,
        out_specs=[vmem] * 2,
        scratch_shapes=[pltpu.VMEM((SIZE_K, SIZE_K), jnp.float32)],
        cost_estimate=pl.CostEstimate(
            flops=6 * 512 * SIZE_K * SIZE_K, bytes_accessed=5 << 20, transcendentals=0
        ),
        compiler_params=pltpu.CompilerParams(vmem_limit_bytes=24 << 20),
        name="panel",
    )(
        core_index.reshape(1),
        lefts,
        own_half,
        other_half,
        singular.reshape(1, -1),
        singular_cot.reshape(1, -1),
    )


def product_kernel(high, low, rights, out):
    out[...] = dot3((high[...], low[...]), split(rights[...]), ((1,), (1,)))


def product(high, low, rights):
    width = 2 * SIZE_K
    step = 256
    whole = pl.BlockSpec((512, width), lambda i: (0, 0))
    return pl.pallas_call(
        product_kernel,
        out_shape=jax.ShapeDtypeStruct((512, 768), jnp.float32),
        grid=(768 // step,),
        in_specs=[whole, whole, pl.BlockSpec((step, width), lambda i: (i, 0))],
        out_specs=pl.BlockSpec((512, step), lambda i: (0, i)),
        cost_estimate=pl.CostEstimate(
            flops=6 * 512 * 768 * width, bytes_accessed=7 << 20, transcendentals=0
        ),
        compiler_params=pltpu.CompilerParams(vmem_limit_bytes=PRODUCT_LIMIT),
        name="product",
    )(high, low, rights)


def local(left, left_cot, right, right_cot, singular, singular_cot):
    core_index = lax.axis_index("core")
    at_low = lax.axis_index("yl") == 0

    right_pair, left_pair, stacked = pack(left, left_cot, right, right_cot)
    rights = lax.all_gather(right_pair, ROW, axis=0, tiled=True)
    other = shift(left_pair, "yl", 2, 1)
    got = swap(stacked)
    mine = half_core(core_index, stacked, got, singular)
    pieces = lax.all_to_all(mine.reshape(16, 16, SIZE_K), OUTER, 0, 0)

    own = jnp.stack([jnp.where(at_low, left_pair, other), jnp.where(at_low, other, left_pair)])
    below = shift(own, Z, 8, 1)
    pair = jnp.stack([below, own])
    mid_below, mid_above = shift(pair, Z, 8, 2), shift(pair, Z, 8, -2)
    pieces = gather(jnp.sum(pieces, axis=0), "yh", 4)
    pieces = gather(jnp.sum(pieces, axis=0), "zh", 4)
    last_above = shift(mid_above, Z, 8, -2)
    blocks = (below, own, mid_below, mid_above, last_above)
    line = assemble(place_kernel, (8, 2, 16, 1024), lax.axis_index(Z), *blocks)
    line = line.reshape(16, 16, 1024)
    rows = jnp.sum(pieces, axis=0)
    own_half = gather(rows, OUTER, 16).reshape(HALF, SIZE_K)
    other_line = swap(line)
    lefts = assemble(
        merge_kernel, (16, 2, 16, 1024), core_index, line, other_line
    ).reshape(-1, 1024)
    other_half = swap(own_half)
    high, low = panel(core_index, lefts, own_half, other_half, singular, singular_cot)
    return product(high, low, rights)


def solution(mesh):
    fine = Mesh(mesh.devices.reshape(SIZES), ALL)
    placed = (
        P(ROW + COL, None),
        P(ROW + COL, None),
        P(COL + ROW, None),
        P(COL + ROW, None),
        P(),
        P(),
    )
    return jax.shard_map(local, mesh=fine, in_specs=placed, out_specs=P(ROW, COL), check_vma=False)
```
